128 devices in a mesh: task: 4 (over y), shard: 32 (over x, z, core).
Axes of the slice: x: 4, y: 4, z: 4, core: 2. Of those that a mesh axis runs over, the one named last changes fastest.
Arguments:
- tokens: bfloat16 [4096, 4096], P(('task', 'shard')), may hold values from -600 to 600
- gain: float32 [4096], replicated, may hold values from 0.5 to 1.5
- task_ids: int32 [4096], P(('task', 'shard')), may hold values from 0 to 7, as said below
- order: int32 [4096], P(('task', 'shard')), may hold values from 0 to 31, as said below
- w_gate: bfloat16 [8, 4096, 14336], P('task', None, 'shard'), may hold values from -0.09375 to 0.09375
- w_up: bfloat16 [8, 4096, 14336], P('task', None, 'shard'), may hold values from -0.09375 to 0.09375
- w_down: bfloat16 [8, 14336, 4096], P('task', 'shard'), may hold values from -0.046875 to 0.046875
Outputs:
- mixed: bfloat16 [4096, 4096], P(('task', 'shard'))
The draws below stay inside these ranges and needn't reach their ends.
Inputs may be any that keep to these rules, and one draw needn't show every extreme that they name: `task_ids`: in each aligned block of 32 rows (the rows of one device) at most 8 rows name any one task; one task, the same for all blocks, is named by exactly 8 rows of every block. `order`: each aligned block of 32 entries is a permutation of 0 to 31.
All inputs are finite; a program needn't handle non-finite values.
Results may differ from the reference program's by a relative error of at most 0.015.
Values may be sent and summed in bfloat16 or wider, within the bound.
No kernel may reach another device: no remote copies, remote signals or barrier semaphores. Data moves between devices by JAX's collectives and lax.ppermute only.
A program may use at most 128 MiB of HBM per device.

```python
import math
import jax
import jax.numpy as jnp
from jax import lax

D = 4096
FF = 14336
TOK_DEV = 32
CAP = 8
EXPERTS = 8
TOKENS = 4096
N_SHARD = 32


def draw_tokens(key, part):
    base_key, row_key, col_key = jax.random.split(jax.random.fold_in(key, 7), 3)
    base = jax.random.normal(base_key, (TOKENS, D), jnp.float32)
    base = jnp.clip(base, -6.0, 6.0)
    row_scale = jnp.exp(jax.random.uniform(row_key, (TOKENS, 1), jnp.float32) * math.log(10.0))
    col_scale = jnp.exp(jax.random.uniform(col_key, (1, D), jnp.float32) * math.log(10.0))
    return (base * row_scale * col_scale).astype(jnp.bfloat16)


def draw_task_ids(key, part):
    block_total = TOKENS // TOK_DEV
    heavy_key, block_key = jax.random.split(jax.random.fold_in(key, 101))
    heavy = jax.random.randint(heavy_key, (), 0, EXPERTS).astype(jnp.int32)
    labels = jnp.repeat(jnp.arange(EXPERTS - 1, dtype=jnp.int32), CAP)

    def one_block(single_key):
        choose_key, shuffle_key = jax.random.split(single_key)
        chosen = jax.random.permutation(choose_key, labels)[:TOK_DEV - CAP]
        others = jnp.where(chosen >= heavy, chosen + 1, chosen).astype(jnp.int32)
        filled = jnp.concatenate([jnp.full((CAP,), heavy, jnp.int32), others])
        return jax.random.permutation(shuffle_key, filled)
    blocks = jax.vmap(one_block)(jax.random.split(block_key, block_total))
    return blocks.reshape(TOKENS).astype(jnp.int32)


def draw_order(key, part):
    block_total = TOKENS // TOK_DEV
    base_key = jax.random.fold_in(key, 202)
    natural = jnp.arange(TOK_DEV, dtype=jnp.int32)

    def one_block(single_key):
        return jax.random.permutation(single_key, natural)
    blocks = jax.vmap(one_block)(jax.random.split(base_key, block_total))
    return blocks.reshape(TOKENS).astype(jnp.int32)


def level_of(stream_key, dims, pieces, smallest, top_value):
    def one(axis_at, shards_of):
        heights = jax.random.uniform(jax.random.fold_in(jax.random.fold_in(stream_key, 6), axis_at), (shards_of,), jnp.float32, smallest / len(pieces), top_value / len(pieces))
        return jnp.repeat(jnp.exp(heights), dims[axis_at] // shards_of).reshape((-1,) + (1,) * (len(dims) - axis_at - 1))

    level = one(*pieces[0])
    for cut in pieces[1:]:
        level = level * one(*cut)
    return level


def gaussian(own_key, dims, scale, bound, cuts=(), kind=jnp.bfloat16):
    drawn = jax.random.normal(own_key, dims, jnp.float32) * scale
    if len(cuts) > 0:
        drawn = level_of(own_key, dims, cuts, -0.22, 0.18) * drawn
    return jnp.clip(drawn, min=-bound, max=bound).astype(kind)


def setup_inputs(seed: int = 0) -> dict:
    arg_keys = jax.random.split(jax.random.key(seed), 8)
    return {
        "tokens": draw_tokens(jax.random.fold_in(arg_keys[7], 71), 0),
        "gain": jnp.clip(1.0 + 0.1 * jax.random.normal(arg_keys[1], (D,), jnp.float32), 0.5, 1.5),
        "task_ids": draw_task_ids(jax.random.fold_in(arg_keys[7], 71), 0),
        "order": draw_order(jax.random.fold_in(arg_keys[7], 71), 0),
        "w_gate": gaussian(arg_keys[4], (EXPERTS, D, FF), D ** -0.5, 0.09375, ((0, 4), (2, 32))),
        "w_up": gaussian(arg_keys[5], (EXPERTS, D, FF), D ** -0.5, 0.09375, ((0, 4), (2, 32))),
        "w_down": gaussian(arg_keys[6], (EXPERTS, FF, D), FF ** -0.5, 0.046875, ((0, 4), (1, 32))),
    }


def expert_rows(operand):
    rows_in, gate_weights, up_weights, down_weights = operand
    gate_value = jnp.dot(rows_in, gate_weights, preferred_element_type=jnp.float32)
    up_value = jnp.dot(rows_in, up_weights, preferred_element_type=jnp.float32)
    hidden = (jax.nn.silu(gate_value) * up_value).astype(jnp.bfloat16)
    row_total = hidden.shape[0]
    hidden_blocks = jnp.swapaxes(hidden.reshape(row_total, N_SHARD, FF // N_SHARD), 0, 1)
    down_blocks = down_weights.reshape(N_SHARD, FF // N_SHARD, D)

    def add_term(running, pair):
        term = jnp.dot(pair[0], pair[1], preferred_element_type=jnp.float32).astype(jnp.bfloat16)
        term = lax.optimization_barrier(term).astype(jnp.float32)
        return (running + term, None)
    start_sum = jnp.zeros((row_total, D), jnp.float32)
    summed, unused = lax.scan(add_term, start_sum, (hidden_blocks, down_blocks))
    return summed.astype(jnp.bfloat16)

def reference(tokens, gain, task_ids, order, w_gate, w_up, w_down):
    values = tokens.astype(jnp.float32)
    mean_square = lax.optimization_barrier(jnp.mean(values * values, axis=-1, keepdims=True))
    normed = (values * lax.rsqrt(mean_square + 1e-06) * gain).astype(jnp.bfloat16)
    block_total = TOKENS // TOK_DEV
    onehot = (task_ids[:, None] == jnp.arange(EXPERTS, dtype=jnp.int32)[None, :]).astype(jnp.int32)
    counted = jnp.cumsum(onehot.reshape(block_total, TOK_DEV, EXPERTS), axis=1).reshape(TOKENS, EXPERTS)
    position = (lax.optimization_barrier(jnp.sum(counted * onehot, axis=1)) - 1).astype(jnp.int32)
    block_index = (jnp.arange(TOKENS, dtype=jnp.int32) // TOK_DEV).astype(jnp.int32)
    per_expert = block_total * CAP
    slot_index = (task_ids * per_expert + block_index * CAP + position).astype(jnp.int32)
    buffered = jnp.zeros((EXPERTS * per_expert, D), jnp.bfloat16).at[slot_index].set(normed)
    buffered = buffered.reshape(EXPERTS, per_expert, D)
    served = lax.map(expert_rows, (buffered, w_gate, w_up, w_down))
    expert_out = served.reshape(EXPERTS * per_expert, D)[slot_index]
    source_rows = (block_index * TOK_DEV + order).astype(jnp.int32)
    return expert_out[source_rows]
```

```python
import functools
import jax
import jax.numpy as jnp
from jax import lax
from jax.experimental import pallas as pl
from jax.experimental.pallas import tpu as pltpu
from jax.sharding import Mesh, PartitionSpec as P

CAP = 8
RING = 4
CORES = 2
EPSILON = 1e-06
F32 = jnp.float32
BF16 = jnp.bfloat16


def shift(v, axis, step):
    return lax.ppermute(v, axis, [(i, (i + step) % RING) for i in range(RING)])


def swap_cores(v):
    return lax.ppermute(v, "core", [(0, 1), (1, 0)])


def ffn_kernel(rows, chunk, core_ref, *refs):
    n = len(rows)
    xs, (wg, wu, wp, wd, wd2), outs = refs[:n], refs[n : n + 5], refs[n + 5 : 2 * n + 5]
    x, w1, w2, gu, h, y, xsem, wsem, ysem = refs[2 * n + 5 :]
    core = core_ref[0]
    part = wd2.shape[0]
    width = wd2.shape[1]
    hidden = CORES * part
    starts = [sum(rows[:i]) for i in range(n)]
    x_copies = [
        pltpu.make_async_copy(xs[i], x.at[pl.ds(starts[i], rows[i])], xsem.at[i]) for i in range(n)
    ]
    w_copies = [
        pltpu.make_async_copy(wg.at[core], w1.at[pl.ds(0, part)], wsem.at[0]),
        pltpu.make_async_copy(wp.at[0], w1.at[pl.ds(part, part)], wsem.at[1]),
        pltpu.make_async_copy(wu.at[core], w1.at[pl.ds(2 * part, part)], wsem.at[2]),
        pltpu.make_async_copy(wp.at[1], w1.at[pl.ds(3 * part, part)], wsem.at[3]),
        pltpu.make_async_copy(wd.at[core], w2.at[pl.ds(0, part)], wsem.at[4]),
        pltpu.make_async_copy(wd2, w2.at[pl.ds(part, part)], wsem.at[5]),
    ]
    for copy in x_copies + w_copies:
        copy.start()
    for copy in x_copies:
        copy.wait()

    @pl.loop(0, 2 * hidden // chunk)
    def _(j):
        for k in range(4):

            @pl.when(j == k * part // chunk)
            def _():
                w_copies[k].wait()

        at = pl.ds(pl.multiple_of(j * chunk, chunk), chunk)
        gu[:, at] = lax.dot_general(
            x[...], w1[at, :], (((1,), (1,)), ((), ())), preferred_element_type=F32
        )

    gate = gu[:, :hidden]
    h[...] = (gate / (1.0 + jnp.exp(-gate)) * gu[:, hidden:]).astype(BF16)
    w_copies[4].wait()
    w_copies[5].wait()

    @pl.loop(0, width // (2 * chunk))
    def _(j):
        cols = pl.ds(pl.multiple_of(j * 2 * chunk, 2 * chunk), 2 * chunk)
        y[:, cols] = jnp.dot(h[...], w2[:, cols], preferred_element_type=F32).astype(BF16)

    y_copies = [
        pltpu.make_async_copy(y.at[pl.ds(starts[i], rows[i])], outs[i], ysem.at[i]) for i in range(n)
    ]
    for copy in y_copies:
        copy.start()
    for copy in y_copies:
        copy.wait()


def ffn(core, xs, weights):
    rows = tuple(v.shape[0] for v in xs)
    total = sum(rows)
    part, width = weights[-1].shape
    any_spec = pl.BlockSpec(memory_space=pl.ANY)
    return pl.pallas_call(
        functools.partial(ffn_kernel, rows, 256),
        out_shape=[jax.ShapeDtypeStruct(v.shape, BF16) for v in xs],
        in_specs=[pl.BlockSpec(memory_space=pltpu.SMEM)] + [any_spec] * (len(xs) + 5),
        out_specs=[any_spec] * len(xs),
        scratch_shapes=[
            pltpu.VMEM((total, width), BF16),
            pltpu.VMEM((2 * CORES * part, width), BF16),
            pltpu.VMEM((CORES * part, width), BF16),
            pltpu.VMEM((total, 2 * CORES * part), F32),
            pltpu.VMEM((total, CORES * part), BF16),
            pltpu.VMEM((total, width), BF16),
            pltpu.SemaphoreType.DMA((len(xs),)),
            pltpu.SemaphoreType.DMA((6,)),
            pltpu.SemaphoreType.DMA((len(xs),)),
        ],
        compiler_params=pltpu.CompilerParams(vmem_limit_bytes=40 * 1024 * 1024),
        cost_estimate=pl.CostEstimate(
            flops=2 * total * width * part * 6,
            transcendentals=total * part * 2,
            bytes_accessed=2 * (6 * width * part + 2 * total * width),
        ),
        name="ffn",
    )(core, *xs, *weights)


def gather_step(v, axis):
    return shift(v, axis, 1), shift(v, axis, -1)


def gather_far(plus, minus, axis):
    half = plus.shape[0] // 2
    return shift(plus[:half], axis, 1), shift(minus[half:], axis, -1)


def ring_gather(v, axis):
    plus, minus = gather_step(v, axis)
    plus2, minus2 = gather_far(plus, minus, axis)
    return jnp.concatenate([v, plus, minus, plus2, minus2], axis=0)


def add(*terms):
    total = terms[0].astype(F32)
    for term in terms[1:]:
        total = total + term.astype(F32)
    return total.astype(BF16)


def scatter_far(plus, minus, plus2, minus2, axis):
    half = plus.shape[0] // 2
    from_next = shift(plus2, axis, -1)
    from_last = shift(minus2, axis, 1)
    plus = jnp.concatenate([add(plus[:half], from_next), plus[half:]], axis=0)
    minus = jnp.concatenate([minus[:half], add(minus[half:], from_last)], axis=0)
    return plus, minus


def scatter_near(own, plus, minus, axis):
    return add(own, shift(plus, axis, -1), shift(minus, axis, 1))


def ring_scatter(v, axis):
    unit = v.shape[0] // RING
    half = unit // 2
    own, plus, minus = v[:unit], v[unit : 2 * unit], v[2 * unit : 3 * unit]
    plus2, minus2 = v[3 * unit : 3 * unit + half], v[3 * unit + half :]
    plus, minus = scatter_far(plus, minus, plus2, minus2, axis)
    return scatter_near(own, plus, minus, axis)


def shards(tokens, gain, task_ids, order, w_gate, w_up, w_down):
    local_experts = w_gate.shape[0]
    expert_count = RING * local_experts
    width = tokens.shape[1]
    group = lax.axis_index("task")
    core = lax.axis_index("core")

    values = tokens.astype(F32)
    mean_square = jnp.mean(values * values, axis=-1, keepdims=True)
    normed = (values * lax.rsqrt(mean_square + EPSILON) * gain).astype(BF16)
    onehot = (task_ids[:, None] == jnp.arange(expert_count, dtype=jnp.int32)[None, :]).astype(
        jnp.int32
    )
    position = jnp.sum(jnp.cumsum(onehot, axis=0) * onehot, axis=1) - 1
    far = (task_ids // local_experts - group) % RING
    other = (task_ids + core) % CORES
    slot_index = (far * CORES + other) * CAP + position
    slot_count = expert_count * CAP
    slot_range = jnp.arange(slot_count, dtype=jnp.int32)
    placing = (slot_index[:, None] == slot_range[None, :]).astype(BF16)
    outgoing = jnp.einsum("rs,rd->sd", placing, normed, preferred_element_type=F32).astype(BF16)
    outgoing = outgoing.reshape(RING, CORES * CAP, width)

    arrived = jnp.stack(
        [outgoing[0]] + [shift(outgoing[k], "task", k) for k in range(1, RING)], axis=0
    ).reshape(RING, CORES, CAP, width)
    rows_a = arrived[:, 0].reshape(RING * CAP, width)
    rows_b = swap_cores(arrived[:, 1].reshape(RING * CAP, width))

    def other_expert(w):
        return lax.dynamic_index_in_dim(w, 1 - core, 0, keepdims=False)

    w_gate = jnp.swapaxes(w_gate, 1, 2)
    w_up = jnp.swapaxes(w_up, 1, 2)
    peer_in = swap_cores(jnp.stack([other_expert(w_gate), other_expert(w_up)], axis=0))
    peer_out = swap_cores(other_expert(w_down))
    weights = (w_gate, w_up, peer_in, w_down, peer_out)
    core_arg = core.astype(jnp.int32).reshape(1)

    a0 = ring_gather(rows_a, "x")
    b0 = ring_gather(rows_b, "z")
    ap, am = gather_step(a0, "z")
    bp, bm = gather_step(b0, "x")
    ap2, am2 = gather_far(ap, am, "z")
    bp2, bm2 = gather_far(bp, bm, "x")

    ya0, yb0 = ffn(core_arg, (a0, b0), weights)
    yap, yam, ybp, ybm = ffn(core_arg, (ap, am, bp, bm), weights)
    yap2, yam2, ybp2, ybm2 = ffn(core_arg, (ap2, am2, bp2, bm2), weights)

    yap, yam = scatter_far(yap, yam, yap2, yam2, "z")
    ybp, ybm = scatter_far(ybp, ybm, ybp2, ybm2, "x")
    ya = scatter_near(ya0, yap, yam, "z")
    yb = scatter_near(yb0, ybp, ybm, "x")
    done_a = ring_scatter(ya, "x")
    done_b = swap_cores(ring_scatter(yb, "z"))

    results = jnp.stack(
        [done_a.reshape(RING, CAP, width), done_b.reshape(RING, CAP, width)], axis=1
    ).reshape(RING, CORES * CAP, width)
    returned = jnp.stack(
        [results[0]] + [shift(results[k], "task", -k) for k in range(1, RING)], axis=0
    ).reshape(slot_count, width)
    wanted = jnp.take(slot_index, order)
    selecting = (wanted[:, None] == slot_range[None, :]).astype(BF16)
    return jnp.dot(selecting, returned, preferred_element_type=F32).astype(BF16)


def solution(mesh):
    devices = mesh.devices.reshape(RING, RING, RING, CORES)
    fine = Mesh(devices, ("task", "x", "z", "core"))
    shard = ("x", "z", "core")
    every = ("task",) + shard
    placed = (
        P(every, None),
        P(),
        P(every),
        P(every),
        P("task", None, shard),
        P("task", None, shard),
        P("task", shard, None),
    )
    return jax.shard_map(
        shards, mesh=fine, in_specs=placed, out_specs=P(every, None), check_vma=False
    )
```

```python
import functools
import jax
import jax.numpy as jnp
from jax import lax
from jax.experimental import pallas as pl
from jax.experimental.pallas import tpu as pltpu
from jax.sharding import Mesh, PartitionSpec as P

CAP = 8
RING = 4
CORES = 2
EPSILON = 1e-06
F32 = jnp.float32
BF16 = jnp.bfloat16


def shift(v, axis, step):
    return lax.ppermute(v, axis, [(i, (i + step) % RING) for i in range(RING)])


def swap_cores(v):
    return lax.ppermute(v, "core", [(0, 1), (1, 0)])


CHUNK = 256
WIDE = 1024
ANYWHERE = pl.BlockSpec(memory_space=pl.ANY)
IN_VMEM = pl.BlockSpec(memory_space=pltpu.VMEM)


def in_vmem(v):
    return pltpu.with_memory_space_constraint(v, pltpu.VMEM)


def in_hbm(v):
    return pltpu.with_memory_space_constraint(v, pltpu.HBM)


def run_copies(copies):
    for copy in copies:
        copy.start()
    for copy in copies:
        copy.wait()


def pick_kernel(which_ref, wg, wu, wd, og, ou, od, sem):
    which = which_ref[0]
    run_copies(
        [
            pltpu.make_async_copy(w.at[which], o, sem.at[i])
            for i, (w, o) in enumerate(((wg, og), (wu, ou), (wd, od)))
        ]
    )


def pick(which, w_gate, w_up, w_down):
    return pl.pallas_call(
        pick_kernel,
        out_shape=[pltpu.VMEM(w.shape[1:], BF16) for w in (w_gate, w_up, w_down)],
        in_specs=[pl.BlockSpec(memory_space=pltpu.SMEM)] + [ANYWHERE] * 3,
        out_specs=[IN_VMEM] * 3,
        scratch_shapes=[pltpu.SemaphoreType.DMA((3,))],
        compiler_params=pltpu.CompilerParams(vmem_limit_bytes=1024 * 1024),
        name="pick",
    )(which, in_hbm(w_gate), in_hbm(w_up), in_hbm(w_down))


def load_kernel(core_ref, wg, wpg, wu, wpu, wd, wpd, w1, w2, sem):
    core = core_ref[0]
    part = wpd.shape[0]
    run_copies(
        [
            pltpu.make_async_copy(wg.at[core], w1.at[pl.ds(0, part)], sem.at[0]),
            pltpu.make_async_copy(wpg, w1.at[pl.ds(part, part)], sem.at[1]),
            pltpu.make_async_copy(wu.at[core], w1.at[pl.ds(2 * part, part)], sem.at[2]),
            pltpu.make_async_copy(wpu, w1.at[pl.ds(3 * part, part)], sem.at[3]),
            pltpu.make_async_copy(wd.at[core], w2.at[pl.ds(0, part)], sem.at[4]),
            pltpu.make_async_copy(wpd, w2.at[pl.ds(part, part)], sem.at[5]),
        ]
    )


def load(core, *weights):
    part, width = weights[-1].shape
    return pl.pallas_call(
        load_kernel,
        out_shape=[
            pltpu.VMEM((2 * CORES * part, width), BF16),
            pltpu.VMEM((CORES * part, width), BF16),
        ],
        in_specs=[pl.BlockSpec(memory_space=pltpu.SMEM)] + [ANYWHERE] * 6,
        out_specs=[IN_VMEM] * 2,
        scratch_shapes=[pltpu.SemaphoreType.DMA((6,))],
        compiler_params=pltpu.CompilerParams(vmem_limit_bytes=1024 * 1024),
        name="load",
    )(core, *[in_hbm(w) if w.ndim == 3 else in_vmem(w) for w in weights])


def ffn_kernel(rows, *refs):
    n = len(rows)
    xs, (w1, w2), outs = refs[:n], refs[n : n + 2], refs[n + 2 : 2 * n + 2]
    x, gu, h = refs[2 * n + 2 :]
    width = w1.shape[1]
    hidden = w2.shape[0]
    starts = [sum(rows[:i]) for i in range(n)]
    for i in range(n):
        x[starts[i] : starts[i] + rows[i], :] = xs[i][...]
    for j in range(2 * hidden // CHUNK):
        at = slice(j * CHUNK, (j + 1) * CHUNK)
        gu[:, at] = lax.dot_general(
            x[...], w1[at, :], (((1,), (1,)), ((), ())), preferred_element_type=F32
        )
    gate = gu[:, :hidden]
    h[...] = (gate / (1.0 + jnp.exp(-gate)) * gu[:, hidden:]).astype(BF16)

    @pl.loop(0, width // WIDE)
    def _(j):
        cols = pl.ds(pl.multiple_of(j * WIDE, WIDE), WIDE)
        y = jnp.dot(h[...], w2[:, cols], preferred_element_type=F32).astype(BF16)
        for i in range(n):
            outs[i][:, cols] = y[starts[i] : starts[i] + rows[i]]


def ffn(xs, w1, w2):
    rows = tuple(v.shape[0] for v in xs)
    total = sum(rows)
    hidden, width = w2.shape
    n = len(xs)
    return pl.pallas_call(
        functools.partial(ffn_kernel, rows),
        out_shape=[pltpu.VMEM(v.shape, BF16) for v in xs],
        in_specs=[IN_VMEM] * (n + 2),
        out_specs=[IN_VMEM] * n,
        scratch_shapes=[
            pltpu.VMEM((total, width), BF16),
            pltpu.VMEM((total, 2 * hidden), F32),
            pltpu.VMEM((total, hidden), BF16),
        ],
        compiler_params=pltpu.CompilerParams(vmem_limit_bytes=10 * 1024 * 1024),
        cost_estimate=pl.CostEstimate(
            flops=6 * total * width * hidden, transcendentals=total * hidden, bytes_accessed=0
        ),
        name="ffn",
    )(*[in_vmem(v) for v in xs], in_vmem(w1), in_vmem(w2))


def gather_step(v, axis):
    return shift(v, axis, 1), shift(v, axis, -1)


def gather_far(plus, minus, axis):
    half = plus.shape[0] // 2
    return shift(plus[:half], axis, 1), shift(minus[half:], axis, -1)


def ring_gather(v, axis):
    plus, minus = gather_step(v, axis)
    plus2, minus2 = gather_far(plus, minus, axis)
    return jnp.concatenate([v, plus, minus, plus2, minus2], axis=0)


def add(*terms):
    total = terms[0].astype(F32)
    for term in terms[1:]:
        total = total + term.astype(F32)
    return total.astype(BF16)


def send_far(plus2, minus2, axis):
    return shift(plus2, axis, -1), shift(minus2, axis, 1)


def add_far(plus, minus, from_next, from_last):
    half = plus.shape[0] // 2
    plus = jnp.concatenate([add(plus[:half], from_next), plus[half:]], axis=0)
    minus = jnp.concatenate([minus[:half], add(minus[half:], from_last)], axis=0)
    return plus, minus


def scatter_near(own, plus, minus, axis):
    return add(own, shift(plus, axis, -1), shift(minus, axis, 1))


def ring_scatter(v, axis):
    unit = v.shape[0] // RING
    half = unit // 2
    own, plus, minus = v[:unit], v[unit : 2 * unit], v[2 * unit : 3 * unit]
    plus2, minus2 = v[3 * unit : 3 * unit + half], v[3 * unit + half :]
    plus, minus = add_far(plus, minus, *send_far(plus2, minus2, axis))
    return scatter_near(own, plus, minus, axis)


def shards(tokens, gain, task_ids, order, w_gate, w_up, w_down):
    local_experts = w_gate.shape[0]
    expert_count = RING * local_experts
    width = tokens.shape[1]
    group = lax.axis_index("task")
    core = lax.axis_index("core")

    values = tokens.astype(F32)
    mean_square = jnp.mean(values * values, axis=-1, keepdims=True)
    normed = (values * lax.rsqrt(mean_square + EPSILON) * gain).astype(BF16)
    onehot = (task_ids[:, None] == jnp.arange(expert_count, dtype=jnp.int32)[None, :]).astype(
        jnp.int32
    )
    position = jnp.sum(jnp.cumsum(onehot, axis=0) * onehot, axis=1) - 1
    far = (task_ids // local_experts - group) % RING
    other = (task_ids + core) % CORES
    slot_index = (other * RING + far) * CAP + position
    slot_count = expert_count * CAP
    slot_range = jnp.arange(slot_count, dtype=jnp.int32)
    placing = (slot_index[:, None] == slot_range[None, :]).astype(BF16)
    outgoing = jnp.einsum("rs,rd->sd", placing, normed, preferred_element_type=F32).astype(BF16)
    per_core = slot_count // CORES
    kept, swapped = outgoing[:per_core], swap_cores(outgoing[per_core:])

    w_gate = jnp.swapaxes(w_gate, 1, 2)
    w_up = jnp.swapaxes(w_up, 1, 2)
    core_arg = core.astype(jnp.int32).reshape(1)
    sent = pick(1 - core_arg, w_gate, w_up, w_down)
    swapped, *sent = lax.optimization_barrier((swapped, *sent))
    peer_gate, peer_up, peer_down = [swap_cores(w) for w in sent]

    def for_group(k):
        at = slice(k * CAP, (k + 1) * CAP)
        return jnp.concatenate([kept[at], swapped[at]], axis=0)

    groups = [for_group(0)] + [shift(for_group(k), "task", k) for k in range(1, RING)]
    a0 = ring_gather(jnp.concatenate(groups[:2], axis=0), "x")
    b0 = ring_gather(jnp.concatenate(groups[2:], axis=0), "z")
    ap, am = gather_step(a0, "z")
    bp, bm = gather_step(b0, "x")
    a0, b0, peer_gate, peer_up, peer_down = lax.optimization_barrier(
        (a0, b0, peer_gate, peer_up, peer_down)
    )
    w1, w2 = load(core_arg, w_gate, peer_gate, w_up, peer_up, w_down, peer_down)
    ya0, yb0 = ffn((a0, b0), w1, w2)
    ap, am, bp, bm, ya0, yb0 = lax.optimization_barrier((ap, am, bp, bm, ya0, yb0))
    far_a = gather_far(ap, am, "z")
    far_b = gather_far(bp, bm, "x")
    yap, ybp = ffn((ap, bp), w1, w2)
    ap2, am2, bp2, bm2, yap, ybp = lax.optimization_barrier((*far_a, *far_b, yap, ybp))
    yap2, yam2, ybp2, ybm2 = ffn((ap2, am2, bp2, bm2), w1, w2)
    yap2, yam2, ybp2, ybm2, am, bm = lax.optimization_barrier((yap2, yam2, ybp2, ybm2, am, bm))
    far_a = send_far(yap2, yam2, "z")
    far_b = send_far(ybp2, ybm2, "x")
    yam, ybm = ffn((am, bm), w1, w2)
    *far_a, yam = lax.optimization_barrier((*far_a, yam))
    *far_b, ybm = lax.optimization_barrier((*far_b, ybm))
    ya = scatter_near(ya0, *add_far(yap, yam, *far_a), "z")
    yb = scatter_near(yb0, *add_far(ybp, ybm, *far_b), "x")
    done_a = ring_scatter(ya, "x")
    done_b = ring_scatter(yb, "z")

    both = 2 * CAP
    groups = [done_a[:both], done_a[both:], done_b[:both], done_b[both:]]
    groups = [groups[0]] + [shift(groups[k], "task", -k) for k in range(1, RING)]
    kept = jnp.concatenate([v[:CAP] for v in groups], axis=0)
    swapped = swap_cores(jnp.concatenate([v[CAP:] for v in groups], axis=0))
    wanted = jnp.take(slot_index, order)
    selecting = (wanted[:, None] == slot_range[None, :]).astype(BF16)
    returned = jnp.concatenate([kept, swapped], axis=0)
    return jnp.dot(selecting, returned, preferred_element_type=F32).astype(BF16)


def solution(mesh):
    devices = mesh.devices.reshape(RING, RING, RING, CORES)
    fine = Mesh(devices, ("task", "x", "z", "core"))
    shard = ("x", "z", "core")
    every = ("task",) + shard
    placed = (
        P(every, None),
        P(),
        P(every),
        P(every),
        P("task", None, shard),
        P("task", None, shard),
        P("task", shard, None),
    )
    return jax.shard_map(
        shards, mesh=fine, in_specs=placed, out_specs=P(every, None), check_vma=False
    )
```

```python
import functools
import jax
import jax.numpy as jnp
from jax import lax
from jax.experimental import pallas as pl
from jax.experimental.pallas import tpu as pltpu
from jax.sharding import Mesh, PartitionSpec as P

CAP = 8
RING = 4
CORES = 2
EPSILON = 1e-06
F32 = jnp.float32
BF16 = jnp.bfloat16


def shift(v, axis, step):
    return lax.ppermute(v, axis, [(i, (i + step) % RING) for i in range(RING)])


def swap_cores(v):
    return lax.ppermute(v, "core", [(0, 1), (1, 0)])


CHUNK = 256
WIDE = 1024
ANYWHERE = pl.BlockSpec(memory_space=pl.ANY)
IN_VMEM = pl.BlockSpec(memory_space=pltpu.VMEM)


def in_vmem(v):
    return pltpu.with_memory_space_constraint(v, pltpu.VMEM)


def in_hbm(v):
    return pltpu.with_memory_space_constraint(v, pltpu.HBM)


def run_copies(copies):
    for copy in copies:
        copy.start()
    for copy in copies:
        copy.wait()


def pick_kernel(which_ref, wg, wu, wd, og, ou, od, sem):
    which = which_ref[0]
    run_copies(
        [
            pltpu.make_async_copy(w.at[which], o, sem.at[i])
            for i, (w, o) in enumerate(((wg, og), (wu, ou), (wd, od)))
        ]
    )


def pick(which, w_gate, w_up, w_down):
    return pl.pallas_call(
        pick_kernel,
        out_shape=[pltpu.VMEM(w.shape[1:], BF16) for w in (w_gate, w_up, w_down)],
        in_specs=[pl.BlockSpec(memory_space=pltpu.SMEM)] + [ANYWHERE] * 3,
        out_specs=[IN_VMEM] * 3,
        scratch_shapes=[pltpu.SemaphoreType.DMA((3,))],
        compiler_params=pltpu.CompilerParams(vmem_limit_bytes=1024 * 1024),
        name="pick",
    )(which, in_hbm(w_gate), in_hbm(w_up), in_hbm(w_down))


def load_kernel(core_ref, wg, wpg, wu, wpu, wd, wpd, w1, w2, sem):
    core = core_ref[0]
    part = wpd.shape[0]
    run_copies(
        [
            pltpu.make_async_copy(wg.at[core], w1.at[pl.ds(0, part)], sem.at[0]),
            pltpu.make_async_copy(wpg, w1.at[pl.ds(part, part)], sem.at[1]),
            pltpu.make_async_copy(wu.at[core], w1.at[pl.ds(2 * part, part)], sem.at[2]),
            pltpu.make_async_copy(wpu, w1.at[pl.ds(3 * part, part)], sem.at[3]),
            pltpu.make_async_copy(wd.at[core], w2.at[pl.ds(0, part)], sem.at[4]),
            pltpu.make_async_copy(wpd, w2.at[pl.ds(part, part)], sem.at[5]),
        ]
    )


def load(core, *weights):
    part, width = weights[-1].shape
    return pl.pallas_call(
        load_kernel,
        out_shape=[
            pltpu.VMEM((2 * CORES * part, width), BF16),
            pltpu.VMEM((CORES * part, width), BF16),
        ],
        in_specs=[pl.BlockSpec(memory_space=pltpu.SMEM)] + [ANYWHERE] * 6,
        out_specs=[IN_VMEM] * 2,
        scratch_shapes=[pltpu.SemaphoreType.DMA((6,))],
        compiler_params=pltpu.CompilerParams(vmem_limit_bytes=1024 * 1024),
        name="load",
    )(core, *[in_hbm(w) if w.ndim == 3 else in_vmem(w) for w in weights])


def ffn_kernel(rows, looped, *refs):
    n = len(rows)
    xs, (w1, w2), outs = refs[:n], refs[n : n + 2], refs[n + 2 : 2 * n + 2]
    x, gu, h = refs[2 * n + 2 :]
    width = w1.shape[1]
    hidden = w2.shape[0]
    starts = [sum(rows[:i]) for i in range(n)]
    for i in range(n):
        x[starts[i] : starts[i] + rows[i], :] = xs[i][...]

    def gate_and_up(at):
        gu[:, at] = lax.dot_general(
            x[...], w1[at, :], (((1,), (1,)), ((), ())), preferred_element_type=F32
        )

    if looped:

        @pl.loop(0, 2 * hidden // CHUNK)
        def _(j):
            gate_and_up(pl.ds(pl.multiple_of(j * CHUNK, CHUNK), CHUNK))

    else:
        for j in range(2 * hidden // CHUNK):
            gate_and_up(slice(j * CHUNK, (j + 1) * CHUNK))

    gate = gu[:, :hidden]
    h[...] = (gate / (1.0 + jnp.exp(-gate)) * gu[:, hidden:]).astype(BF16)

    @pl.loop(0, width // WIDE)
    def _(j):
        cols = pl.ds(pl.multiple_of(j * WIDE, WIDE), WIDE)
        y = jnp.dot(h[...], w2[:, cols], preferred_element_type=F32).astype(BF16)
        for i in range(n):
            outs[i][:, cols] = y[starts[i] : starts[i] + rows[i]]


def ffn(xs, w1, w2, looped=False):
    rows = tuple(v.shape[0] for v in xs)
    total = sum(rows)
    hidden, width = w2.shape
    n = len(xs)
    return pl.pallas_call(
        functools.partial(ffn_kernel, rows, looped),
        out_shape=[pltpu.VMEM(v.shape, BF16) for v in xs],
        in_specs=[IN_VMEM] * (n + 2),
        out_specs=[IN_VMEM] * n,
        scratch_shapes=[
            pltpu.VMEM((total, width), BF16),
            pltpu.VMEM((total, 2 * hidden), F32),
            pltpu.VMEM((total, hidden), BF16),
        ],
        compiler_params=pltpu.CompilerParams(vmem_limit_bytes=10 * 1024 * 1024),
        cost_estimate=pl.CostEstimate(
            flops=6 * total * width * hidden, transcendentals=total * hidden, bytes_accessed=0
        ),
        name="ffn",
    )(*[in_vmem(v) for v in xs], in_vmem(w1), in_vmem(w2))


def ring_gather(v, axis):
    half = v.shape[0] // 2
    plus, minus = shift(v, axis, 1), shift(v, axis, -1)
    plus2, minus2 = shift(plus[:half], axis, 1), shift(minus[half:], axis, -1)
    return jnp.concatenate([v, plus, minus, plus2, minus2], axis=0)


def add(*terms):
    total = terms[0].astype(F32)
    for term in terms[1:]:
        total = total + term.astype(F32)
    return total.astype(BF16)


def ring_scatter(v, axis):
    unit = v.shape[0] // RING
    half = unit // 2
    own, plus, minus = v[:unit], v[unit : 2 * unit], v[2 * unit : 3 * unit]
    plus2, minus2 = v[3 * unit : 3 * unit + half], v[3 * unit + half :]
    from_next, from_last = shift(plus2, axis, -1), shift(minus2, axis, 1)
    plus = jnp.concatenate([add(plus[:half], from_next), plus[half:]], axis=0)
    minus = jnp.concatenate([minus[:half], add(minus[half:], from_last)], axis=0)
    return add(own, shift(plus, axis, -1), shift(minus, axis, 1))


def first_halves(v, axis):
    half = v.shape[0] // 2
    return [shift(v[:half], axis, 1), shift(v[half:], axis, -1)]


def second_halves(v, axis):
    half = v.shape[0] // 2
    return [shift(v[half:], axis, 1), shift(v[:half], axis, -1)]


def onward(pair, axis):
    return [shift(pair[0], axis, 1), shift(pair[1], axis, -1)]


def backward(pair, axis):
    return [shift(pair[0], axis, -1), shift(pair[1], axis, 1)]


def after(*lists):
    flat = lax.optimization_barrier([v for part in lists for v in part])
    cut, out = 0, []
    for part in lists:
        out.append(flat[cut : cut + len(part)])
        cut += len(part)
    return out


def collect(own, early, late):
    half = own.shape[0] // 2
    return jnp.concatenate(
        [add(own[:half], early[1], late[0]), add(own[half:], early[0], late[1])], axis=0
    )


def layer(tokens, gain, task_ids, order, w_gate, w_up, w_down):
    local_experts = w_gate.shape[0]
    expert_count = RING * local_experts
    group = lax.axis_index("task")
    core = lax.axis_index("core")

    values = tokens.astype(F32)
    mean_square = jnp.mean(values * values, axis=-1, keepdims=True)
    normed = (values * lax.rsqrt(mean_square + EPSILON) * gain).astype(BF16)
    onehot = (task_ids[:, None] == jnp.arange(expert_count, dtype=jnp.int32)[None, :]).astype(
        jnp.int32
    )
    position = jnp.sum(jnp.cumsum(onehot, axis=0) * onehot, axis=1) - 1
    far = (task_ids // local_experts - group) % RING
    other = (task_ids + core) % CORES
    slot_index = (other * RING + far) * CAP + position
    slot_count = expert_count * CAP
    slot_range = jnp.arange(slot_count, dtype=jnp.int32)
    placing = (slot_index[:, None] == slot_range[None, :]).astype(BF16)
    outgoing = jnp.einsum("rs,rd->sd", placing, normed, preferred_element_type=F32).astype(BF16)
    per_core = slot_count // CORES
    kept, swapped = outgoing[:per_core], swap_cores(outgoing[per_core:])

    w_gate = jnp.swapaxes(w_gate, 1, 2)
    w_up = jnp.swapaxes(w_up, 1, 2)
    core_arg = core.astype(jnp.int32).reshape(1)
    swapped, which = lax.optimization_barrier((swapped, 1 - core_arg))
    sent = pick(which, w_gate, w_up, w_down)
    peers = [swap_cores(w) for w in sent]

    def for_group(k):
        at = slice(k * CAP, (k + 1) * CAP)
        return jnp.concatenate([kept[at], swapped[at]], axis=0)

    groups = [for_group(0)] + [shift(for_group(k), "task", k) for k in range(1, RING)]
    a0 = ring_gather(jnp.concatenate(groups[:2], axis=0), "x")
    b0 = ring_gather(jnp.concatenate(groups[2:], axis=0), "z")
    lead_a, lead_b = first_halves(a0, "z"), first_halves(b0, "x")
    rest_a, rest_b = second_halves(a0, "z"), second_halves(b0, "x")
    (a0, b0), peers = after([a0, b0], peers)
    w1, w2 = load(core_arg, w_gate, peers[0], w_up, peers[1], w_down, peers[2])
    (w1, w2), lead_a, lead_b = after([w1, w2], lead_a, lead_b)
    far_a, far_b = onward(lead_a, "z"), onward(lead_b, "x")
    y0 = ffn([a0, b0], w1, w2, looped=True)
    y0, rest_a, rest_b = after(y0, rest_a, rest_b)
    early = ffn(rest_a + rest_b, w1, w2)
    early, far_a, far_b = after(early, far_a, far_b)
    early_a, early_b = backward(early[:2], "z"), backward(early[2:], "x")
    far = ffn(far_a + far_b, w1, w2)
    far, lead_a, lead_b = after(far, lead_a, lead_b)
    far_a, far_b = backward(far[:2], "z"), backward(far[2:], "x")
    late = ffn(lead_a + lead_b, w1, w2)
    far_a, late_a = after(far_a, late[:2])
    far_b, late_b = after(far_b, late[2:])
    late_a = backward([add(v, w) for v, w in zip(late_a, far_a)], "z")
    late_b = backward([add(v, w) for v, w in zip(late_b, far_b)], "x")
    ya = collect(y0[0], early_a, late_a)
    yb = collect(y0[1], early_b, late_b)
    done_a = ring_scatter(ya, "x")
    done_b = ring_scatter(yb, "z")

    both = 2 * CAP
    groups = [done_a[:both], done_a[both:], done_b[:both], done_b[both:]]
    groups = [groups[0]] + [shift(groups[k], "task", -k) for k in range(1, RING)]
    kept = jnp.concatenate([v[:CAP] for v in groups], axis=0)
    swapped = swap_cores(jnp.concatenate([v[CAP:] for v in groups], axis=0))
    wanted = jnp.take(slot_index, order)
    selecting = (wanted[:, None] == slot_range[None, :]).astype(BF16)
    returned = jnp.concatenate([kept, swapped], axis=0)
    return jnp.dot(selecting, returned, preferred_element_type=F32).astype(BF16)


def solution(mesh):
    devices = mesh.devices.reshape(RING, RING, RING, CORES)
    fine = Mesh(devices, ("task", "x", "z", "core"))
    shard = ("x", "z", "core")
    every = ("task",) + shard
    placed = (
        P(every, None),
        P(),
        P(every),
        P(every),
        P("task", None, shard),
        P("task", None, shard),
        P("task", shard, None),
    )
    return jax.shard_map(
        layer, mesh=fine, in_specs=placed, out_specs=P(every, None), check_vma=False
    )
```

```python
import functools
import jax
import jax.numpy as jnp
from jax import lax
from jax.experimental import pallas as pl
from jax.experimental.pallas import tpu as pltpu
from jax.sharding import Mesh, PartitionSpec as P

CAP = 8
RING = 4
CORES = 2
EPSILON = 1e-06
F32 = jnp.float32
BF16 = jnp.bfloat16


def shift(v, step):
    return lax.ppermute(v, "task", [(i, (i + step) % RING) for i in range(RING)])


def hop(v, phase, step):
    pairs = []
    for x in range(RING):
        for z in range(RING):
            for core in range(CORES):
                on_x = (core == 0) == (phase == 1)
                to_x = (x + step * on_x) % RING
                to_z = (z + step * (not on_x)) % RING
                source = (x * RING + z) * CORES + core
                pairs.append((source, (to_x * RING + to_z) * CORES + core))
    return lax.ppermute(v, ("x", "z", "core"), pairs)


def swap_cores(v):
    return lax.ppermute(v, "core", [(0, 1), (1, 0)])


CHUNK = 256
WIDE = 1024
ANYWHERE = pl.BlockSpec(memory_space=pl.ANY)
IN_VMEM = pl.BlockSpec(memory_space=pltpu.VMEM)


def in_vmem(v):
    return pltpu.with_memory_space_constraint(v, pltpu.VMEM)


def in_hbm(v):
    return pltpu.with_memory_space_constraint(v, pltpu.HBM)


def run_copies(copies):
    for copy in copies:
        copy.start()
    for copy in copies:
        copy.wait()


def pick_kernel(which_ref, wg, wu, wd, og, ou, od, sem):
    which = which_ref[0]
    run_copies(
        [
            pltpu.make_async_copy(w.at[which], o, sem.at[i])
            for i, (w, o) in enumerate(((wg, og), (wu, ou), (wd, od)))
        ]
    )


def pick(which, w_gate, w_up, w_down):
    return pl.pallas_call(
        pick_kernel,
        out_shape=[pltpu.VMEM(w.shape[1:], BF16) for w in (w_gate, w_up, w_down)],
        in_specs=[pl.BlockSpec(memory_space=pltpu.SMEM)] + [ANYWHERE] * 3,
        out_specs=[IN_VMEM] * 3,
        scratch_shapes=[pltpu.SemaphoreType.DMA((3,))],
        compiler_params=pltpu.CompilerParams(vmem_limit_bytes=1024 * 1024),
        name="pick",
    )(which, in_hbm(w_gate), in_hbm(w_up), in_hbm(w_down))


def load_kernel(core_ref, wg, wpg, wu, wpu, wd, wpd, w1, w2, sem):
    core = core_ref[0]
    part = wpd.shape[0]
    run_copies(
        [
            pltpu.make_async_copy(wg.at[core], w1.at[pl.ds(0, part)], sem.at[0]),
            pltpu.make_async_copy(wpg, w1.at[pl.ds(part, part)], sem.at[1]),
            pltpu.make_async_copy(wu.at[core], w1.at[pl.ds(2 * part, part)], sem.at[2]),
            pltpu.make_async_copy(wpu, w1.at[pl.ds(3 * part, part)], sem.at[3]),
            pltpu.make_async_copy(wd.at[core], w2.at[pl.ds(0, part)], sem.at[4]),
            pltpu.make_async_copy(wpd, w2.at[pl.ds(part, part)], sem.at[5]),
        ]
    )


def load(core, *weights):
    part, width = weights[-1].shape
    return pl.pallas_call(
        load_kernel,
        out_shape=[
            pltpu.VMEM((2 * CORES * part, width), BF16),
            pltpu.VMEM((CORES * part, width), BF16),
        ],
        in_specs=[pl.BlockSpec(memory_space=pltpu.SMEM)] + [ANYWHERE] * 6,
        out_specs=[IN_VMEM] * 2,
        scratch_shapes=[pltpu.SemaphoreType.DMA((6,))],
        compiler_params=pltpu.CompilerParams(vmem_limit_bytes=1024 * 1024),
        name="load",
    )(core, *[in_hbm(w) if w.ndim == 3 else in_vmem(w) for w in weights])


def ffn_kernel(rows, looped, *refs):
    n = len(rows)
    xs, (w1, w2), outs = refs[:n], refs[n : n + 2], refs[n + 2 : 2 * n + 2]
    x, gu, h = refs[2 * n + 2 :]
    width = w1.shape[1]
    hidden = w2.shape[0]
    starts = [sum(rows[:i]) for i in range(n)]
    for i in range(n):
        x[starts[i] : starts[i] + rows[i], :] = xs[i][...]

    def gate_and_up(at):
        gu[:, at] = lax.dot_general(
            x[...], w1[at, :], (((1,), (1,)), ((), ())), preferred_element_type=F32
        )

    if looped:

        @pl.loop(0, 2 * hidden // CHUNK)
        def _(j):
            gate_and_up(pl.ds(pl.multiple_of(j * CHUNK, CHUNK), CHUNK))

    else:
        for j in range(2 * hidden // CHUNK):
            gate_and_up(slice(j * CHUNK, (j + 1) * CHUNK))

    gate = gu[:, :hidden]
    h[...] = (gate / (1.0 + jnp.exp(-gate)) * gu[:, hidden:]).astype(BF16)

    @pl.loop(0, width // WIDE)
    def _(j):
        cols = pl.ds(pl.multiple_of(j * WIDE, WIDE), WIDE)
        y = jnp.dot(h[...], w2[:, cols], preferred_element_type=F32).astype(BF16)
        for i in range(n):
            outs[i][:, cols] = y[starts[i] : starts[i] + rows[i]]


def ffn(xs, w1, w2, looped=False):
    rows = tuple(v.shape[0] for v in xs)
    total = sum(rows)
    hidden, width = w2.shape
    n = len(xs)
    return pl.pallas_call(
        functools.partial(ffn_kernel, rows, looped),
        out_shape=[pltpu.VMEM(v.shape, BF16) for v in xs],
        in_specs=[IN_VMEM] * (n + 2),
        out_specs=[IN_VMEM] * n,
        scratch_shapes=[
            pltpu.VMEM((total, width), BF16),
            pltpu.VMEM((total, 2 * hidden), F32),
            pltpu.VMEM((total, hidden), BF16),
        ],
        compiler_params=pltpu.CompilerParams(vmem_limit_bytes=10 * 1024 * 1024),
        cost_estimate=pl.CostEstimate(
            flops=6 * total * width * hidden, transcendentals=total * hidden, bytes_accessed=0
        ),
        name="ffn",
    )(*[in_vmem(v) for v in xs], in_vmem(w1), in_vmem(w2))


def ring_gather(v, phase):
    half = v.shape[0] // 2
    plus, minus = hop(v, phase, 1), hop(v, phase, -1)
    plus2, minus2 = hop(plus[:half], phase, 1), hop(minus[half:], phase, -1)
    return jnp.concatenate([v, plus, minus, plus2, minus2], axis=0)


def add(*terms):
    total = terms[0].astype(F32)
    for term in terms[1:]:
        total = total + term.astype(F32)
    return total.astype(BF16)


def ring_scatter(v, phase):
    unit = v.shape[0] // RING
    half = unit // 2
    own, plus, minus = v[:unit], v[unit : 2 * unit], v[2 * unit : 3 * unit]
    plus2, minus2 = v[3 * unit : 3 * unit + half], v[3 * unit + half :]
    from_next, from_last = hop(plus2, phase, -1), hop(minus2, phase, 1)
    plus = jnp.concatenate([add(plus[:half], from_next), plus[half:]], axis=0)
    minus = jnp.concatenate([minus[:half], add(minus[half:], from_last)], axis=0)
    return add(own, hop(plus, phase, -1), hop(minus, phase, 1))


def first_halves(v, phase):
    half = v.shape[0] // 2
    return [hop(v[:half], phase, 1), hop(v[half:], phase, -1)]


def second_halves(v, phase):
    half = v.shape[0] // 2
    return [hop(v[half:], phase, 1), hop(v[:half], phase, -1)]


def onward(pair, phase):
    return [hop(pair[0], phase, 1), hop(pair[1], phase, -1)]


def backward(pair, phase):
    return [hop(pair[0], phase, -1), hop(pair[1], phase, 1)]


def after(*lists):
    flat = lax.optimization_barrier([v for part in lists for v in part])
    cut, out = 0, []
    for part in lists:
        out.append(flat[cut : cut + len(part)])
        cut += len(part)
    return out


def collect(own, early, late):
    half = own.shape[0] // 2
    return jnp.concatenate(
        [add(own[:half], early[1], late[0]), add(own[half:], early[0], late[1])], axis=0
    )


def layer(tokens, gain, task_ids, order, w_gate, w_up, w_down):
    local_experts = w_gate.shape[0]
    expert_count = RING * local_experts
    group = lax.axis_index("task")
    core = lax.axis_index("core")

    values = tokens.astype(F32)
    mean_square = jnp.mean(values * values, axis=-1, keepdims=True)
    normed = (values * lax.rsqrt(mean_square + EPSILON) * gain).astype(BF16)
    onehot = (task_ids[:, None] == jnp.arange(expert_count, dtype=jnp.int32)[None, :]).astype(
        jnp.int32
    )
    position = jnp.sum(jnp.cumsum(onehot, axis=0) * onehot, axis=1) - 1
    far = (task_ids // local_experts - group) % RING
    other = (task_ids + core) % CORES
    slot_index = (other * RING + far) * CAP + position
    slot_count = expert_count * CAP
    slot_range = jnp.arange(slot_count, dtype=jnp.int32)
    placing = (slot_index[:, None] == slot_range[None, :]).astype(BF16)
    outgoing = jnp.einsum("rs,rd->sd", placing, normed, preferred_element_type=F32).astype(BF16)
    per_core = slot_count // CORES
    kept, swapped = outgoing[:per_core], swap_cores(outgoing[per_core:])

    w_gate = jnp.swapaxes(w_gate, 1, 2)
    w_up = jnp.swapaxes(w_up, 1, 2)
    core_arg = core.astype(jnp.int32).reshape(1)
    swapped, which = lax.optimization_barrier((swapped, 1 - core_arg))
    sent = pick(which, w_gate, w_up, w_down)
    peers = [swap_cores(w) for w in sent]

    def for_group(k):
        at = slice(k * CAP, (k + 1) * CAP)
        return jnp.concatenate([kept[at], swapped[at]], axis=0)

    groups = [for_group(0)] + [shift(for_group(k), k) for k in range(1, RING)]
    rows = ring_gather(jnp.concatenate(groups, axis=0), 1)
    lead = first_halves(rows, 2)
    rest = second_halves(rows, 2)
    (rows,), peers = after([rows], peers)
    w1, w2 = load(core_arg, w_gate, peers[0], w_up, peers[1], w_down, peers[2])
    (w1, w2), lead = after([w1, w2], lead)
    far = onward(lead, 2)
    own = ffn([rows], w1, w2)
    own, rest = after(own, rest)
    early = ffn(rest, w1, w2)
    early, far = after(early, far)
    early = backward(early, 2)
    far = ffn(far, w1, w2)
    far, lead = after(far, lead)
    far = backward(far, 2)
    late = ffn(lead, w1, w2)
    far, late = after(far, late)
    late = backward([add(v, w) for v, w in zip(late, far)], 2)
    done = ring_scatter(collect(own[0], early, late), 1)

    both = CORES * CAP
    groups = [done[k * both : (k + 1) * both] for k in range(RING)]
    groups = [groups[0]] + [shift(groups[k], -k) for k in range(1, RING)]
    kept = jnp.concatenate([v[:CAP] for v in groups], axis=0)
    swapped = swap_cores(jnp.concatenate([v[CAP:] for v in groups], axis=0))
    wanted = jnp.take(slot_index, order)
    selecting = (wanted[:, None] == slot_range[None, :]).astype(BF16)
    returned = jnp.concatenate([kept, swapped], axis=0)
    return jnp.dot(selecting, returned, preferred_element_type=F32).astype(BF16)


def solution(mesh):
    devices = mesh.devices.reshape(RING, RING, RING, CORES)
    fine = Mesh(devices, ("task", "x", "z", "core"))
    shard = ("x", "z", "core")
    every = ("task",) + shard
    placed = (
        P(every, None),
        P(),
        P(every),
        P(every),
        P("task", None, shard),
        P("task", None, shard),
        P("task", shard, None),
    )
    return jax.shard_map(
        layer, mesh=fine, in_specs=placed, out_specs=P(every, None), check_vma=False
    )
```

```python
import functools
import jax
import jax.numpy as jnp
from jax import lax
from jax.experimental import pallas as pl
from jax.experimental.pallas import tpu as pltpu
from jax.sharding import Mesh, PartitionSpec as P

CAP = 8
RING = 4
CORES = 2
EPSILON = 1e-06
F32 = jnp.float32
BF16 = jnp.bfloat16


def shift(v, axis, step):
    return lax.ppermute(v, axis, [(i, (i + step) % RING) for i in range(RING)])


def swap_cores(v):
    return lax.ppermute(v, "core", [(0, 1), (1, 0)])


CHUNK = 256
WIDE = 1024
ANYWHERE = pl.BlockSpec(memory_space=pl.ANY)
IN_VMEM = pl.BlockSpec(memory_space=pltpu.VMEM)


def in_vmem(v):
    return pltpu.with_memory_space_constraint(v, pltpu.VMEM)


def in_hbm(v):
    return pltpu.with_memory_space_constraint(v, pltpu.HBM)


def run_copies(copies):
    for copy in copies:
        copy.start()
    for copy in copies:
        copy.wait()


def dispatch_kernel(
    task_hbm, order_hbm, tokens_hbm, gain_hbm, out, select, tokens, gain, task_ref, order_ref,
    count, slot, sem,
):
    sources = (task_hbm, order_hbm, tokens_hbm, gain_hbm)
    places = (task_ref, order_ref, tokens, gain)
    copies = [
        pltpu.make_async_copy(v, w, sem.at[i]) for i, (v, w) in enumerate(zip(sources, places))
    ]
    for copy in copies:
        copy.start()
    group = lax.axis_index("task")
    core = lax.axis_index("core")
    rows = tokens.shape[0]
    slots = out.shape[0]
    experts = count.shape[0]
    for e in range(experts):
        count[e] = 0
    copies[0].wait()
    lanes = lax.broadcasted_iota(jnp.int32, (slots, rows), 1)
    targets = jnp.zeros((slots, rows), jnp.int32)
    for r in range(rows):
        task = task_ref[r]
        position = count[task]
        count[task] = position + 1
        far = (task // CORES - group) & (RING - 1)
        other = (task + core) & (CORES - 1)
        at = (other * RING + far) * CAP + position
        slot[r] = at
        targets = jnp.where(lanes == r, at, targets)
    placing = (lax.broadcasted_iota(jnp.int32, (slots, rows), 0) == targets).astype(BF16)
    copies[2].wait()
    copies[3].wait()
    values = tokens[...].astype(F32)
    mean_square = jnp.mean(values * values, axis=-1, keepdims=True)
    normed = (values * lax.rsqrt(mean_square + EPSILON) * gain[...]).astype(BF16)
    out[...] = jnp.dot(placing, normed, preferred_element_type=F32).astype(BF16)
    copies[1].wait()
    sublanes = lax.broadcasted_iota(jnp.int32, (rows, slots), 0)
    wanted = jnp.zeros((rows, slots), jnp.int32)
    for r in range(rows):
        wanted = jnp.where(sublanes == r, slot[order_ref[r]], wanted)
    chosen = lax.broadcasted_iota(jnp.int32, (rows, slots), 1) == wanted
    select[...] = chosen.astype(BF16)


def dispatch(task_ids, order, tokens, gain, experts):
    rows, width = tokens.shape
    slots = experts * CAP
    arrays = (task_ids, order, tokens, gain.reshape(1, width))
    return pl.pallas_call(
        dispatch_kernel,
        out_shape=[pltpu.VMEM((slots, width), BF16), pltpu.VMEM((rows, slots), BF16)],
        in_specs=[ANYWHERE] * 4,
        out_specs=[IN_VMEM] * 2,
        scratch_shapes=[
            pltpu.VMEM((rows, width), BF16),
            pltpu.VMEM((1, width), F32),
            pltpu.SMEM((rows,), jnp.int32),
            pltpu.SMEM((rows,), jnp.int32),
            pltpu.SMEM((experts,), jnp.int32),
            pltpu.SMEM((rows,), jnp.int32),
            pltpu.SemaphoreType.DMA((4,)),
        ],
        compiler_params=pltpu.CompilerParams(vmem_limit_bytes=8 * 1024 * 1024),
        name="dispatch",
    )(*[in_hbm(v) for v in arrays])


def pick_kernel(which_ref, wg, wu, wd, og, ou, od, sem):
    which = which_ref[0]
    run_copies(
        [
            pltpu.make_async_copy(w.at[which], o, sem.at[i])
            for i, (w, o) in enumerate(((wg, og), (wu, ou), (wd, od)))
        ]
    )


def pick(which, w_gate, w_up, w_down):
    return pl.pallas_call(
        pick_kernel,
        out_shape=[pltpu.VMEM(w.shape[1:], BF16) for w in (w_gate, w_up, w_down)],
        in_specs=[pl.BlockSpec(memory_space=pltpu.SMEM)] + [ANYWHERE] * 3,
        out_specs=[IN_VMEM] * 3,
        scratch_shapes=[pltpu.SemaphoreType.DMA((3,))],
        compiler_params=pltpu.CompilerParams(vmem_limit_bytes=1024 * 1024),
        name="pick",
    )(which, in_hbm(w_gate), in_hbm(w_up), in_hbm(w_down))


def load_kernel(core_ref, wg, wpg, wu, wpu, wd, wpd, w1, w2, sem):
    core = core_ref[0]
    part = wpd.shape[0]
    run_copies(
        [
            pltpu.make_async_copy(wg.at[core], w1.at[pl.ds(0, part)], sem.at[0]),
            pltpu.make_async_copy(wpg, w1.at[pl.ds(part, part)], sem.at[1]),
            pltpu.make_async_copy(wu.at[core], w1.at[pl.ds(2 * part, part)], sem.at[2]),
            pltpu.make_async_copy(wpu, w1.at[pl.ds(3 * part, part)], sem.at[3]),
            pltpu.make_async_copy(wd.at[core], w2.at[pl.ds(0, part)], sem.at[4]),
            pltpu.make_async_copy(wpd, w2.at[pl.ds(part, part)], sem.at[5]),
        ]
    )


def load(core, *weights):
    part, width = weights[-1].shape
    return pl.pallas_call(
        load_kernel,
        out_shape=[
            pltpu.VMEM((2 * CORES * part, width), BF16),
            pltpu.VMEM((CORES * part, width), BF16),
        ],
        in_specs=[pl.BlockSpec(memory_space=pltpu.SMEM)] + [ANYWHERE] * 6,
        out_specs=[IN_VMEM] * 2,
        scratch_shapes=[pltpu.SemaphoreType.DMA((6,))],
        compiler_params=pltpu.CompilerParams(vmem_limit_bytes=1024 * 1024),
        name="load",
    )(core, *[in_hbm(w) if w.ndim == 3 else in_vmem(w) for w in weights])


def ffn_kernel(rows, looped, *refs):
    n = len(rows)
    xs, (w1, w2), outs = refs[:n], refs[n : n + 2], refs[n + 2 : 2 * n + 2]
    x, gu, h = refs[2 * n + 2 :]
    width = w1.shape[1]
    hidden = w2.shape[0]
    starts = [sum(rows[:i]) for i in range(n)]
    for i in range(n):
        x[starts[i] : starts[i] + rows[i], :] = xs[i][...]

    def gate_and_up(at):
        gu[:, at] = lax.dot_general(
            x[...], w1[at, :], (((1,), (1,)), ((), ())), preferred_element_type=F32
        )

    if looped:

        @pl.loop(0, 2 * hidden // CHUNK)
        def _(j):
            gate_and_up(pl.ds(pl.multiple_of(j * CHUNK, CHUNK), CHUNK))

    else:
        for j in range(2 * hidden // CHUNK):
            gate_and_up(slice(j * CHUNK, (j + 1) * CHUNK))

    gate = gu[:, :hidden]
    h[...] = (gate / (1.0 + jnp.exp(-gate)) * gu[:, hidden:]).astype(BF16)

    @pl.loop(0, width // WIDE)
    def _(j):
        cols = pl.ds(pl.multiple_of(j * WIDE, WIDE), WIDE)
        y = jnp.dot(h[...], w2[:, cols], preferred_element_type=F32).astype(BF16)
        for i in range(n):
            outs[i][:, cols] = y[starts[i] : starts[i] + rows[i]]


def ffn(xs, w1, w2, looped=False):
    rows = tuple(v.shape[0] for v in xs)
    total = sum(rows)
    hidden, width = w2.shape
    n = len(xs)
    return pl.pallas_call(
        functools.partial(ffn_kernel, rows, looped),
        out_shape=[pltpu.VMEM(v.shape, BF16) for v in xs],
        in_specs=[IN_VMEM] * (n + 2),
        out_specs=[IN_VMEM] * n,
        scratch_shapes=[
            pltpu.VMEM((total, width), BF16),
            pltpu.VMEM((total, 2 * hidden), F32),
            pltpu.VMEM((total, hidden), BF16),
        ],
        compiler_params=pltpu.CompilerParams(vmem_limit_bytes=10 * 1024 * 1024),
        cost_estimate=pl.CostEstimate(
            flops=6 * total * width * hidden, transcendentals=total * hidden, bytes_accessed=0
        ),
        name="ffn",
    )(*[in_vmem(v) for v in xs], in_vmem(w1), in_vmem(w2))


def ring_gather(v, axis):
    half = v.shape[0] // 2
    plus, minus = shift(v, axis, 1), shift(v, axis, -1)
    plus2, minus2 = shift(plus[:half], axis, 1), shift(minus[half:], axis, -1)
    return jnp.concatenate([v, plus, minus, plus2, minus2], axis=0)


def add(*terms):
    total = terms[0].astype(F32)
    for term in terms[1:]:
        total = total + term.astype(F32)
    return total.astype(BF16)


def ring_scatter(v, axis):
    unit = v.shape[0] // RING
    half = unit // 2
    own, plus, minus = v[:unit], v[unit : 2 * unit], v[2 * unit : 3 * unit]
    plus2, minus2 = v[3 * unit : 3 * unit + half], v[3 * unit + half :]
    from_next, from_last = shift(plus2, axis, -1), shift(minus2, axis, 1)
    plus = jnp.concatenate([add(plus[:half], from_next), plus[half:]], axis=0)
    minus = jnp.concatenate([minus[:half], add(minus[half:], from_last)], axis=0)
    return add(own, shift(plus, axis, -1), shift(minus, axis, 1))


def first_halves(v, axis):
    half = v.shape[0] // 2
    return [shift(v[:half], axis, 1), shift(v[half:], axis, -1)]


def second_halves(v, axis):
    half = v.shape[0] // 2
    return [shift(v[half:], axis, 1), shift(v[:half], axis, -1)]


def onward(pair, axis):
    return [shift(pair[0], axis, 1), shift(pair[1], axis, -1)]


def backward(pair, axis):
    return [shift(pair[0], axis, -1), shift(pair[1], axis, 1)]


def after(*lists):
    flat = lax.optimization_barrier([v for part in lists for v in part])
    cut, out = 0, []
    for part in lists:
        out.append(flat[cut : cut + len(part)])
        cut += len(part)
    return out


def collect(own, early, late):
    half = own.shape[0] // 2
    return jnp.concatenate(
        [add(own[:half], early[1], late[0]), add(own[half:], early[0], late[1])], axis=0
    )


def layer(tokens, gain, task_ids, order, w_gate, w_up, w_down):
    local_experts = w_gate.shape[0]
    expert_count = RING * local_experts
    core = lax.axis_index("core")

    core_arg = core.astype(jnp.int32).reshape(1)
    outgoing, selecting = dispatch(task_ids, order, tokens, gain, expert_count)
    slot_count = expert_count * CAP
    per_core = slot_count // CORES
    kept, swapped = outgoing[:per_core], swap_cores(outgoing[per_core:])

    w_gate = jnp.swapaxes(w_gate, 1, 2)
    w_up = jnp.swapaxes(w_up, 1, 2)
    swapped, which = lax.optimization_barrier((swapped, 1 - core_arg))
    sent = pick(which, w_gate, w_up, w_down)
    peers = [swap_cores(w) for w in sent]

    def for_group(k):
        at = slice(k * CAP, (k + 1) * CAP)
        return jnp.concatenate([kept[at], swapped[at]], axis=0)

    groups = [for_group(0)] + [shift(for_group(k), "task", k) for k in range(1, RING)]
    a0 = ring_gather(jnp.concatenate(groups[:2], axis=0), "x")
    b0 = ring_gather(jnp.concatenate(groups[2:], axis=0), "z")
    lead_a, lead_b = first_halves(a0, "z"), first_halves(b0, "x")
    rest_a, rest_b = second_halves(a0, "z"), second_halves(b0, "x")
    (a0, b0), peers = after([a0, b0], peers)
    w1, w2 = load(core_arg, w_gate, peers[0], w_up, peers[1], w_down, peers[2])
    (w1, w2), lead_a, lead_b = after([w1, w2], lead_a, lead_b)
    far_a, far_b = onward(lead_a, "z"), onward(lead_b, "x")
    early = ffn(rest_a + rest_b, w1, w2)
    early_a, early_b = backward(early[:2], "z"), backward(early[2:], "x")
    far = ffn(far_a + far_b, w1, w2)
    far, lead_a, lead_b = after(far, lead_a, lead_b)
    far_a, far_b = backward(far[:2], "z"), backward(far[2:], "x")
    late = ffn(lead_a + lead_b, w1, w2)
    far_a, late_a = after(far_a, late[:2])
    far_b, late_b, (a0, b0) = after(far_b, late[2:], [a0, b0])
    late_a = backward([add(v, w) for v, w in zip(late_a, far_a)], "z")
    late_b = backward([add(v, w) for v, w in zip(late_b, far_b)], "x")
    y0 = ffn([a0, b0], w1, w2, looped=True)
    ya = collect(y0[0], early_a, late_a)
    yb = collect(y0[1], early_b, late_b)
    done_a = ring_scatter(ya, "x")
    done_b = ring_scatter(yb, "z")

    both = 2 * CAP
    groups = [done_a[:both], done_a[both:], done_b[:both], done_b[both:]]
    groups = [groups[0]] + [shift(groups[k], "task", -k) for k in range(1, RING)]
    kept = jnp.concatenate([v[:CAP] for v in groups], axis=0)
    swapped = swap_cores(jnp.concatenate([v[CAP:] for v in groups], axis=0))
    returned = jnp.concatenate([kept, swapped], axis=0)
    return jnp.dot(selecting, returned, preferred_element_type=F32).astype(BF16)


def solution(mesh):
    devices = mesh.devices.reshape(RING, RING, RING, CORES)
    fine = Mesh(devices, ("task", "x", "z", "core"))
    shard = ("x", "z", "core")
    every = ("task",) + shard
    placed = (
        P(every, None),
        P(),
        P(every),
        P(every),
        P("task", None, shard),
        P("task", None, shard),
        P("task", shard, None),
    )
    return jax.shard_map(
        layer, mesh=fine, in_specs=placed, out_specs=P(every, None), check_vma=False
    )
```

```python
import functools
import jax
import jax.numpy as jnp
from jax import lax
from jax.experimental import pallas as pl
from jax.experimental.pallas import tpu as pltpu
from jax.sharding import Mesh, PartitionSpec as P

CAP = 8
RING = 4
CORES = 2
EPSILON = 1e-06
F32 = jnp.float32
BF16 = jnp.bfloat16


def shift(v, axis, step):
    return lax.ppermute(v, axis, [(i, (i + step) % RING) for i in range(RING)])


def swap_cores(v):
    return lax.ppermute(v, "core", [(0, 1), (1, 0)])


CHUNK = 256
WIDE = 1024
ANYWHERE = pl.BlockSpec(memory_space=pl.ANY)
IN_VMEM = pl.BlockSpec(memory_space=pltpu.VMEM)


def in_vmem(v):
    return pltpu.with_memory_space_constraint(v, pltpu.VMEM)


def in_hbm(v):
    return pltpu.with_memory_space_constraint(v, pltpu.HBM)


def run_copies(copies):
    for copy in copies:
        copy.start()
    for copy in copies:
        copy.wait()


def dispatch_kernel(
    task_hbm, order_hbm, tokens_hbm, gain_hbm, out, select, tokens, gain, task_ref, order_ref,
    count, slot, sem,
):
    sources = (task_hbm, order_hbm, tokens_hbm, gain_hbm)
    places = (task_ref, order_ref, tokens, gain)
    copies = [
        pltpu.make_async_copy(v, w, sem.at[i]) for i, (v, w) in enumerate(zip(sources, places))
    ]
    for copy in copies:
        copy.start()
    group = lax.axis_index("task")
    core = lax.axis_index("core")
    rows = tokens.shape[0]
    slots = out.shape[0]
    experts = count.shape[0]
    for e in range(experts):
        count[e] = 0
    copies[0].wait()
    lanes = lax.broadcasted_iota(jnp.int32, (slots, rows), 1)
    targets = jnp.zeros((slots, rows), jnp.int32)
    for r in range(rows):
        task = task_ref[r]
        position = count[task]
        count[task] = position + 1
        far = (task // CORES - group) & (RING - 1)
        other = (task + core) & (CORES - 1)
        at = (other * RING + far) * CAP + position
        slot[r] = at
        targets = jnp.where(lanes == r, at, targets)
    placing = (lax.broadcasted_iota(jnp.int32, (slots, rows), 0) == targets).astype(BF16)
    copies[2].wait()
    copies[3].wait()
    values = tokens[...].astype(F32)
    mean_square = jnp.mean(values * values, axis=-1, keepdims=True)
    normed = (values * lax.rsqrt(mean_square + EPSILON) * gain[...]).astype(BF16)
    out[...] = jnp.dot(placing, normed, preferred_element_type=F32).astype(BF16)
    copies[1].wait()
    sublanes = lax.broadcasted_iota(jnp.int32, (rows, slots), 0)
    wanted = jnp.zeros((rows, slots), jnp.int32)
    for r in range(rows):
        wanted = jnp.where(sublanes == r, slot[order_ref[r]], wanted)
    chosen = lax.broadcasted_iota(jnp.int32, (rows, slots), 1) == wanted
    select[...] = chosen.astype(BF16)


def dispatch(task_ids, order, tokens, gain, experts):
    rows, width = tokens.shape
    slots = experts * CAP
    arrays = (task_ids, order, tokens, gain.reshape(1, width))
    return pl.pallas_call(
        dispatch_kernel,
        out_shape=[pltpu.VMEM((slots, width), BF16), pltpu.VMEM((rows, slots), BF16)],
        in_specs=[ANYWHERE] * 4,
        out_specs=[IN_VMEM] * 2,
        scratch_shapes=[
            pltpu.VMEM((rows, width), BF16),
            pltpu.VMEM((1, width), F32),
            pltpu.SMEM((rows,), jnp.int32),
            pltpu.SMEM((rows,), jnp.int32),
            pltpu.SMEM((experts,), jnp.int32),
            pltpu.SMEM((rows,), jnp.int32),
            pltpu.SemaphoreType.DMA((4,)),
        ],
        compiler_params=pltpu.CompilerParams(vmem_limit_bytes=8 * 1024 * 1024),
        name="dispatch",
    )(*[in_hbm(v) for v in arrays])


def load_kernel(core_ref, wg, wpg, wu, wpu, wd, wpd, w1, w2, sem):
    core = core_ref[0]
    part = wpd.shape[1]
    run_copies(
        [
            pltpu.make_async_copy(wg.at[core], w1.at[pl.ds(0, part)], sem.at[0]),
            pltpu.make_async_copy(wpg.at[core], w1.at[pl.ds(part, part)], sem.at[1]),
            pltpu.make_async_copy(wu.at[core], w1.at[pl.ds(2 * part, part)], sem.at[2]),
            pltpu.make_async_copy(wpu.at[core], w1.at[pl.ds(3 * part, part)], sem.at[3]),
            pltpu.make_async_copy(wd.at[core], w2.at[pl.ds(0, part)], sem.at[4]),
            pltpu.make_async_copy(wpd.at[core], w2.at[pl.ds(part, part)], sem.at[5]),
        ]
    )


def load(core, *weights):
    part, width = weights[-1].shape[1:]
    return pl.pallas_call(
        load_kernel,
        out_shape=[
            pltpu.VMEM((2 * CORES * part, width), BF16),
            pltpu.VMEM((CORES * part, width), BF16),
        ],
        in_specs=[pl.BlockSpec(memory_space=pltpu.SMEM)] + [ANYWHERE] * 6,
        out_specs=[IN_VMEM] * 2,
        scratch_shapes=[pltpu.SemaphoreType.DMA((6,))],
        compiler_params=pltpu.CompilerParams(vmem_limit_bytes=1024 * 1024),
        name="load",
    )(core, *[w if i % 2 else in_hbm(w) for i, w in enumerate(weights)])


def ffn_kernel(rows, looped, *refs):
    n = len(rows)
    xs, (w1, w2), outs = refs[:n], refs[n : n + 2], refs[n + 2 : 2 * n + 2]
    x, gu, h = refs[2 * n + 2 :]
    width = w1.shape[1]
    hidden = w2.shape[0]
    starts = [sum(rows[:i]) for i in range(n)]
    for i in range(n):
        x[starts[i] : starts[i] + rows[i], :] = xs[i][...]

    def gate_and_up(at):
        gu[:, at] = lax.dot_general(
            x[...], w1[at, :], (((1,), (1,)), ((), ())), preferred_element_type=F32
        )

    if looped:

        @pl.loop(0, 2 * hidden // CHUNK)
        def _(j):
            gate_and_up(pl.ds(pl.multiple_of(j * CHUNK, CHUNK), CHUNK))

    else:
        for j in range(2 * hidden // CHUNK):
            gate_and_up(slice(j * CHUNK, (j + 1) * CHUNK))

    gate = gu[:, :hidden]
    h[...] = (gate / (1.0 + jnp.exp(-gate)) * gu[:, hidden:]).astype(BF16)

    @pl.loop(0, width // WIDE)
    def _(j):
        cols = pl.ds(pl.multiple_of(j * WIDE, WIDE), WIDE)
        y = jnp.dot(h[...], w2[:, cols], preferred_element_type=F32).astype(BF16)
        for i in range(n):
            outs[i][:, cols] = y[starts[i] : starts[i] + rows[i]]


def ffn(xs, w1, w2, looped=False):
    rows = tuple(v.shape[0] for v in xs)
    total = sum(rows)
    hidden, width = w2.shape
    n = len(xs)
    return pl.pallas_call(
        functools.partial(ffn_kernel, rows, looped),
        out_shape=[pltpu.VMEM(v.shape, BF16) for v in xs],
        in_specs=[IN_VMEM] * (n + 2),
        out_specs=[IN_VMEM] * n,
        scratch_shapes=[
            pltpu.VMEM((total, width), BF16),
            pltpu.VMEM((total, 2 * hidden), F32),
            pltpu.VMEM((total, hidden), BF16),
        ],
        compiler_params=pltpu.CompilerParams(vmem_limit_bytes=10 * 1024 * 1024),
        cost_estimate=pl.CostEstimate(
            flops=6 * total * width * hidden, transcendentals=total * hidden, bytes_accessed=0
        ),
        name="ffn",
    )(*[in_vmem(v) for v in xs], in_vmem(w1), in_vmem(w2))


def ring_gather(v, axis):
    half = v.shape[0] // 2
    plus, minus = shift(v, axis, 1), shift(v, axis, -1)
    plus2, minus2 = shift(plus[:half], axis, 1), shift(minus[half:], axis, -1)
    return jnp.concatenate([v, plus, minus, plus2, minus2], axis=0)


def add(*terms):
    total = terms[0].astype(F32)
    for term in terms[1:]:
        total = total + term.astype(F32)
    return total.astype(BF16)


def ring_scatter(v, axis):
    unit = v.shape[0] // RING
    half = unit // 2
    own, plus, minus = v[:unit], v[unit : 2 * unit], v[2 * unit : 3 * unit]
    plus2, minus2 = v[3 * unit : 3 * unit + half], v[3 * unit + half :]
    from_next, from_last = shift(plus2, axis, -1), shift(minus2, axis, 1)
    plus = jnp.concatenate([add(plus[:half], from_next), plus[half:]], axis=0)
    minus = jnp.concatenate([minus[:half], add(minus[half:], from_last)], axis=0)
    from_next, from_last = shift(plus, axis, -1), shift(minus, axis, 1)
    return add(own, from_next, from_last)


def first_halves(v, axis):
    half = v.shape[0] // 2
    return [shift(v[:half], axis, 1), shift(v[half:], axis, -1)]


def second_halves(v, axis):
    half = v.shape[0] // 2
    return [shift(v[half:], axis, 1), shift(v[:half], axis, -1)]


def onward(pair, axis):
    return [shift(pair[0], axis, 1), shift(pair[1], axis, -1)]


def backward(pair, axis):
    return [shift(pair[0], axis, -1), shift(pair[1], axis, 1)]


def after(*lists):
    flat = lax.optimization_barrier([v for part in lists for v in part])
    cut, out = 0, []
    for part in lists:
        out.append(flat[cut : cut + len(part)])
        cut += len(part)
    return out


def collect(own, early, late):
    half = own.shape[0] // 2
    return jnp.concatenate(
        [add(own[:half], early[1], late[0]), add(own[half:], early[0], late[1])], axis=0
    )


def layer(tokens, gain, task_ids, order, w_gate, w_up, w_down):
    local_experts = w_gate.shape[0]
    expert_count = RING * local_experts
    core = lax.axis_index("core")

    core_arg = core.astype(jnp.int32).reshape(1)
    outgoing, selecting = dispatch(task_ids, order, tokens, gain, expert_count)
    slot_count = expert_count * CAP
    per_core = slot_count // CORES
    kept, swapped = outgoing[:per_core], swap_cores(outgoing[per_core:])

    w_gate = jnp.swapaxes(w_gate, 1, 2)
    w_up = jnp.swapaxes(w_up, 1, 2)
    swapped, *sent = lax.optimization_barrier((swapped, w_gate, w_up, w_down))
    peers = [swap_cores(w) for w in sent]

    def for_group(k):
        at = slice(k * CAP, (k + 1) * CAP)
        return jnp.concatenate([kept[at], swapped[at]], axis=0)

    groups = [for_group(0)] + [shift(for_group(k), "task", k) for k in range(1, RING)]
    a0 = ring_gather(jnp.concatenate(groups[:2], axis=0), "x")
    b0 = ring_gather(jnp.concatenate(groups[2:], axis=0), "z")
    lead_a, lead_b = first_halves(a0, "z"), first_halves(b0, "x")
    rest_a, rest_b = second_halves(a0, "z"), second_halves(b0, "x")
    (a0, b0), peers = after([a0, b0], peers)
    w1, w2 = load(core_arg, w_gate, peers[0], w_up, peers[1], w_down, peers[2])
    far_a, far_b = onward(lead_a, "z"), onward(lead_b, "x")
    early = ffn(rest_a + rest_b, w1, w2)
    early_a, early_b = backward(early[:2], "z"), backward(early[2:], "x")
    far = ffn(far_a + far_b, w1, w2)
    far, lead_a, lead_b = after(far, lead_a, lead_b)
    far_a, far_b = backward(far[:2], "z"), backward(far[2:], "x")
    late = ffn(lead_a + lead_b, w1, w2)
    far_a, late_a = after(far_a, late[:2])
    far_b, late_b, (a0, b0) = after(far_b, late[2:], [a0, b0])
    late_a = backward([add(v, w) for v, w in zip(late_a, far_a)], "z")
    late_b = backward([add(v, w) for v, w in zip(late_b, far_b)], "x")
    y0 = ffn([a0, b0], w1, w2, looped=True)
    ya = collect(y0[0], early_a, late_a)
    yb = collect(y0[1], early_b, late_b)
    done_a = ring_scatter(ya, "x")
    done_b = ring_scatter(yb, "z")

    both = 2 * CAP
    groups = [done_a[:both], done_a[both:], done_b[:both], done_b[both:]]
    first = shift(groups[1], "task", -1)
    last = [shift(groups[k], "task", -k) for k in range(2, RING)]
    groups = [groups[0], first] + last
    kept = jnp.concatenate([v[:CAP] for v in groups], axis=0)
    swapped = swap_cores(jnp.concatenate([v[CAP:] for v in groups], axis=0))
    returned = jnp.concatenate([kept, swapped], axis=0)
    return jnp.dot(selecting, returned, preferred_element_type=F32).astype(BF16)


def solution(mesh):
    devices = mesh.devices.reshape(RING, RING, RING, CORES)
    fine = Mesh(devices, ("task", "x", "z", "core"))
    shard = ("x", "z", "core")
    every = ("task",) + shard
    placed = (
        P(every, None),
        P(),
        P(every),
        P(every),
        P("task", None, shard),
        P("task", None, shard),
        P("task", shard, None),
    )
    return jax.shard_map(
        layer, mesh=fine, in_specs=placed, out_specs=P(every, None), check_vma=False
    )
```

```python
import functools
import jax
import jax.numpy as jnp
from jax import lax
from jax.experimental import pallas as pl
from jax.experimental.pallas import tpu as pltpu
from jax.sharding import Mesh, PartitionSpec as P

CAP = 8
RING = 4
CORES = 2
EPSILON = 1e-06
F32 = jnp.float32
BF16 = jnp.bfloat16


def shift(v, axis, step):
    return lax.ppermute(v, axis, [(i, (i + step) % RING) for i in range(RING)])


def swap_cores(v):
    return lax.ppermute(v, "core", [(0, 1), (1, 0)])


CHUNK = 256
WIDE = 1024
ANYWHERE = pl.BlockSpec(memory_space=pl.ANY)
IN_VMEM = pl.BlockSpec(memory_space=pltpu.VMEM)


def in_vmem(v):
    return pltpu.with_memory_space_constraint(v, pltpu.VMEM)


def in_hbm(v):
    return pltpu.with_memory_space_constraint(v, pltpu.HBM)


def run_copies(copies):
    for copy in copies:
        copy.start()
    for copy in copies:
        copy.wait()


def dispatch_kernel(
    task_hbm, order_hbm, tokens_hbm, gain_hbm, out, select, tokens, gain, task_ref, order_ref,
    count, slot, sem,
):
    sources = (task_hbm, order_hbm, tokens_hbm, gain_hbm)
    places = (task_ref, order_ref, tokens, gain)
    copies = [
        pltpu.make_async_copy(v, w, sem.at[i]) for i, (v, w) in enumerate(zip(sources, places))
    ]
    for copy in copies:
        copy.start()
    group = lax.axis_index("task")
    core = lax.axis_index("core")
    rows = tokens.shape[0]
    slots = out.shape[0]
    experts = count.shape[0]
    for e in range(experts):
        count[e] = 0
    copies[0].wait()
    lanes = lax.broadcasted_iota(jnp.int32, (slots, rows), 1)
    targets = jnp.zeros((slots, rows), jnp.int32)
    for r in range(rows):
        task = task_ref[r]
        position = count[task]
        count[task] = position + 1
        far = (task // CORES - group) & (RING - 1)
        other = (task + core) & (CORES - 1)
        at = (other * RING + far) * CAP + position
        slot[r] = at
        targets = jnp.where(lanes == r, at, targets)
    placing = (lax.broadcasted_iota(jnp.int32, (slots, rows), 0) == targets).astype(BF16)
    copies[2].wait()
    copies[3].wait()
    values = tokens[...].astype(F32)
    mean_square = jnp.mean(values * values, axis=-1, keepdims=True)
    normed = (values * lax.rsqrt(mean_square + EPSILON) * gain[...]).astype(BF16)
    out[...] = jnp.dot(placing, normed, preferred_element_type=F32).astype(BF16)
    copies[1].wait()
    sublanes = lax.broadcasted_iota(jnp.int32, (rows, slots), 0)
    wanted = jnp.zeros((rows, slots), jnp.int32)
    for r in range(rows):
        wanted = jnp.where(sublanes == r, slot[order_ref[r]], wanted)
    chosen = lax.broadcasted_iota(jnp.int32, (rows, slots), 1) == wanted
    select[...] = chosen.astype(BF16)


def dispatch(task_ids, order, tokens, gain, experts):
    rows, width = tokens.shape
    slots = experts * CAP
    arrays = (task_ids, order, tokens, gain.reshape(1, width))
    return pl.pallas_call(
        dispatch_kernel,
        out_shape=[pltpu.VMEM((slots, width), BF16), pltpu.VMEM((rows, slots), BF16)],
        in_specs=[ANYWHERE] * 4,
        out_specs=[IN_VMEM] * 2,
        scratch_shapes=[
            pltpu.VMEM((rows, width), BF16),
            pltpu.VMEM((1, width), F32),
            pltpu.SMEM((rows,), jnp.int32),
            pltpu.SMEM((rows,), jnp.int32),
            pltpu.SMEM((experts,), jnp.int32),
            pltpu.SMEM((rows,), jnp.int32),
            pltpu.SemaphoreType.DMA((4,)),
        ],
        compiler_params=pltpu.CompilerParams(vmem_limit_bytes=8 * 1024 * 1024),
        name="dispatch",
    )(*[in_hbm(v) for v in arrays])


def pick_kernel(which_ref, wg, wu, wd, og, ou, od, sem):
    which = which_ref[0]
    run_copies(
        [
            pltpu.make_async_copy(w.at[which], o, sem.at[i])
            for i, (w, o) in enumerate(((wg, og), (wu, ou), (wd, od)))
        ]
    )


def pick(which, w_gate, w_up, w_down):
    return pl.pallas_call(
        pick_kernel,
        out_shape=[pltpu.VMEM(w.shape[1:], BF16) for w in (w_gate, w_up, w_down)],
        in_specs=[pl.BlockSpec(memory_space=pltpu.SMEM)] + [ANYWHERE] * 3,
        out_specs=[IN_VMEM] * 3,
        scratch_shapes=[pltpu.SemaphoreType.DMA((3,))],
        compiler_params=pltpu.CompilerParams(vmem_limit_bytes=1024 * 1024),
        name="pick",
    )(which, in_hbm(w_gate), in_hbm(w_up), in_hbm(w_down))


def load_kernel(core_ref, wg, wpg, wu, wpu, wd, wpd, w1, w2, sem):
    core = core_ref[0]
    part = wpd.shape[0]
    run_copies(
        [
            pltpu.make_async_copy(wg.at[core], w1.at[pl.ds(0, part)], sem.at[0]),
            pltpu.make_async_copy(wpg, w1.at[pl.ds(part, part)], sem.at[1]),
            pltpu.make_async_copy(wu.at[core], w1.at[pl.ds(2 * part, part)], sem.at[2]),
            pltpu.make_async_copy(wpu, w1.at[pl.ds(3 * part, part)], sem.at[3]),
            pltpu.make_async_copy(wd.at[core], w2.at[pl.ds(0, part)], sem.at[4]),
            pltpu.make_async_copy(wpd, w2.at[pl.ds(part, part)], sem.at[5]),
        ]
    )


def load(core, *weights):
    part, width = weights[-1].shape
    return pl.pallas_call(
        load_kernel,
        out_shape=[
            pltpu.VMEM((2 * CORES * part, width), BF16),
            pltpu.VMEM((CORES * part, width), BF16),
        ],
        in_specs=[pl.BlockSpec(memory_space=pltpu.SMEM)] + [ANYWHERE] * 6,
        out_specs=[IN_VMEM] * 2,
        scratch_shapes=[pltpu.SemaphoreType.DMA((6,))],
        compiler_params=pltpu.CompilerParams(vmem_limit_bytes=1024 * 1024),
        name="load",
    )(core, *[in_hbm(w) if w.ndim == 3 else in_vmem(w) for w in weights])


def ffn_kernel(rows, looped, *refs):
    n = len(rows)
    xs, (w1, w2), outs = refs[:n], refs[n : n + 2], refs[n + 2 : 2 * n + 2]
    x, gu, h = refs[2 * n + 2 :]
    width = w1.shape[1]
    hidden = w2.shape[0]
    starts = [sum(rows[:i]) for i in range(n)]
    for i in range(n):
        x[starts[i] : starts[i] + rows[i], :] = xs[i][...]

    def gate_and_up(at):
        gu[:, at] = lax.dot_general(
            x[...], w1[at, :], (((1,), (1,)), ((), ())), preferred_element_type=F32
        )

    if looped:

        @pl.loop(0, 2 * hidden // CHUNK)
        def _(j):
            gate_and_up(pl.ds(pl.multiple_of(j * CHUNK, CHUNK), CHUNK))

    else:
        for j in range(2 * hidden // CHUNK):
            gate_and_up(slice(j * CHUNK, (j + 1) * CHUNK))

    gate = gu[:, :hidden]
    h[...] = (gate / (1.0 + jnp.exp(-gate)) * gu[:, hidden:]).astype(BF16)

    @pl.loop(0, width // WIDE)
    def _(j):
        cols = pl.ds(pl.multiple_of(j * WIDE, WIDE), WIDE)
        y = jnp.dot(h[...], w2[:, cols], preferred_element_type=F32).astype(BF16)
        for i in range(n):
            outs[i][:, cols] = y[starts[i] : starts[i] + rows[i]]


def ffn(xs, w1, w2, looped=False):
    rows = tuple(v.shape[0] for v in xs)
    total = sum(rows)
    hidden, width = w2.shape
    n = len(xs)
    return pl.pallas_call(
        functools.partial(ffn_kernel, rows, looped),
        out_shape=[pltpu.VMEM(v.shape, BF16) for v in xs],
        in_specs=[IN_VMEM] * (n + 2),
        out_specs=[IN_VMEM] * n,
        scratch_shapes=[
            pltpu.VMEM((total, width), BF16),
            pltpu.VMEM((total, 2 * hidden), F32),
            pltpu.VMEM((total, hidden), BF16),
        ],
        compiler_params=pltpu.CompilerParams(vmem_limit_bytes=10 * 1024 * 1024),
        cost_estimate=pl.CostEstimate(
            flops=6 * total * width * hidden, transcendentals=total * hidden, bytes_accessed=0
        ),
        name="ffn",
    )(*[in_vmem(v) for v in xs], in_vmem(w1), in_vmem(w2))


def ring_gather(v, axis):
    far, plus, minus = [shift(v, axis, step) for step in (2, 1, -1)]
    return jnp.concatenate([v, plus, minus, far], axis=0)


def add(*terms):
    total = terms[0].astype(F32)
    for term in terms[1:]:
        total = total + term.astype(F32)
    return total.astype(BF16)


def ring_scatter(v, axis):
    unit = v.shape[0] // RING
    own, plus, minus, far = [v[k * unit : (k + 1) * unit] for k in range(RING)]
    far, plus, minus = shift(far, axis, 2), shift(plus, axis, -1), shift(minus, axis, 1)
    return add(own, plus, minus, far)


def first_halves(v, axis):
    half = v.shape[0] // 2
    return [shift(v[:half], axis, 1), shift(v[half:], axis, -1)]


def second_halves(v, axis):
    half = v.shape[0] // 2
    return [shift(v[half:], axis, 1), shift(v[:half], axis, -1)]


def onward(pair, axis):
    return [shift(pair[0], axis, 1), shift(pair[1], axis, -1)]


def backward(pair, axis):
    return [shift(pair[0], axis, -1), shift(pair[1], axis, 1)]


def after(*lists):
    flat = lax.optimization_barrier([v for part in lists for v in part])
    cut, out = 0, []
    for part in lists:
        out.append(flat[cut : cut + len(part)])
        cut += len(part)
    return out


def collect(own, early, late):
    half = own.shape[0] // 2
    return jnp.concatenate(
        [add(own[:half], early[1], late[0]), add(own[half:], early[0], late[1])], axis=0
    )


def layer(tokens, gain, task_ids, order, w_gate, w_up, w_down):
    local_experts = w_gate.shape[0]
    expert_count = RING * local_experts
    core = lax.axis_index("core")

    core_arg = core.astype(jnp.int32).reshape(1)
    outgoing, selecting = dispatch(task_ids, order, tokens, gain, expert_count)
    slot_count = expert_count * CAP
    per_core = slot_count // CORES
    kept, swapped = outgoing[:per_core], swap_cores(outgoing[per_core:])

    w_gate = jnp.swapaxes(w_gate, 1, 2)
    w_up = jnp.swapaxes(w_up, 1, 2)
    swapped, which = lax.optimization_barrier((swapped, 1 - core_arg))
    sent = pick(which, w_gate, w_up, w_down)
    peers = [swap_cores(w) for w in sent]

    def for_group(k):
        at = slice(k * CAP, (k + 1) * CAP)
        return jnp.concatenate([kept[at], swapped[at]], axis=0)

    groups = [for_group(0)] + [shift(for_group(k), "task", k) for k in range(1, RING)]
    a0 = ring_gather(jnp.concatenate(groups[:2], axis=0), "x")
    b0 = ring_gather(jnp.concatenate(groups[2:], axis=0), "z")
    lead_a, lead_b = first_halves(a0, "z"), first_halves(b0, "x")
    rest_a, rest_b = second_halves(a0, "z"), second_halves(b0, "x")
    (a0, b0), peers = after([a0, b0], peers)
    w1, w2 = load(core_arg, w_gate, peers[0], w_up, peers[1], w_down, peers[2])
    far_a, far_b = onward(lead_a, "z"), onward(lead_b, "x")
    early = ffn(rest_a + rest_b, w1, w2)
    early_a, early_b = backward(early[:2], "z"), backward(early[2:], "x")
    far = ffn(far_a + far_b, w1, w2)
    far, lead_a, lead_b = after(far, lead_a, lead_b)
    far_a, far_b = backward(far[:2], "z"), backward(far[2:], "x")
    late = ffn(lead_a + lead_b, w1, w2)
    far_a, late_a = after(far_a, late[:2])
    far_b, late_b, (a0, b0) = after(far_b, late[2:], [a0, b0])
    late_a = backward([add(v, w) for v, w in zip(late_a, far_a)], "z")
    late_b = backward([add(v, w) for v, w in zip(late_b, far_b)], "x")
    y0 = ffn([a0, b0], w1, w2)
    ya = collect(y0[0], early_a, late_a)
    yb = collect(y0[1], early_b, late_b)
    done_a = ring_scatter(ya, "x")
    done_b = ring_scatter(yb, "z")

    both = 2 * CAP
    groups = [done_a[:both], done_a[both:], done_b[:both], done_b[both:]]
    first = shift(groups[1], "task", -1)
    last = [shift(groups[k], "task", -k) for k in range(2, RING)]
    groups = [groups[0], first] + last
    kept = jnp.concatenate([v[:CAP] for v in groups], axis=0)
    swapped = swap_cores(jnp.concatenate([v[CAP:] for v in groups], axis=0))
    returned = jnp.concatenate([kept, swapped], axis=0)
    return jnp.dot(selecting, returned, preferred_element_type=F32).astype(BF16)


def solution(mesh):
    devices = mesh.devices.reshape(RING, RING, RING, CORES)
    fine = Mesh(devices, ("task", "x", "z", "core"))
    shard = ("x", "z", "core")
    every = ("task",) + shard
    placed = (
        P(every, None),
        P(),
        P(every),
        P(every),
        P("task", None, shard),
        P("task", None, shard),
        P("task", shard, None),
    )
    return jax.shard_map(
        layer, mesh=fine, in_specs=placed, out_specs=P(every, None), check_vma=False
    )
```

```python
import functools
import jax
import jax.numpy as jnp
from jax import lax
from jax.experimental import pallas as pl
from jax.experimental.pallas import tpu as pltpu
from jax.sharding import Mesh, PartitionSpec as P

CAP = 8
RING = 4
CORES = 2
EPSILON = 1e-06
F32 = jnp.float32
BF16 = jnp.bfloat16


def shift(v, axis, step):
    return lax.ppermute(v, axis, [(i, (i + step) % RING) for i in range(RING)])


def swap_cores(v):
    return lax.ppermute(v, "core", [(0, 1), (1, 0)])


CHUNK = 256
WIDE = 1024
ANYWHERE = pl.BlockSpec(memory_space=pl.ANY)
IN_VMEM = pl.BlockSpec(memory_space=pltpu.VMEM)


def in_vmem(v):
    return pltpu.with_memory_space_constraint(v, pltpu.VMEM)


def in_hbm(v):
    return pltpu.with_memory_space_constraint(v, pltpu.HBM)


def run_copies(copies):
    for copy in copies:
        copy.start()
    for copy in copies:
        copy.wait()


def dispatch_kernel(
    task_hbm, order_hbm, tokens_hbm, gain_hbm, out, select, tokens, gain, task_ref, order_ref,
    count, slot, sem,
):
    sources = (task_hbm, order_hbm, tokens_hbm, gain_hbm)
    places = (task_ref, order_ref, tokens, gain)
    copies = [
        pltpu.make_async_copy(v, w, sem.at[i]) for i, (v, w) in enumerate(zip(sources, places))
    ]
    for copy in copies:
        copy.start()
    group = lax.axis_index("task")
    core = lax.axis_index("core")
    rows = tokens.shape[0]
    slots = out.shape[0]
    experts = count.shape[0]
    for e in range(experts):
        count[e] = 0
    copies[0].wait()
    lanes = lax.broadcasted_iota(jnp.int32, (slots, rows), 1)
    targets = jnp.zeros((slots, rows), jnp.int32)
    for r in range(rows):
        task = task_ref[r]
        position = count[task]
        count[task] = position + 1
        far = (task // CORES - group) & (RING - 1)
        other = (task + core) & (CORES - 1)
        at = (other * RING + far) * CAP + position
        slot[r] = at
        targets = jnp.where(lanes == r, at, targets)
    placing = (lax.broadcasted_iota(jnp.int32, (slots, rows), 0) == targets).astype(BF16)
    copies[2].wait()
    copies[3].wait()
    values = tokens[...].astype(F32)
    mean_square = jnp.mean(values * values, axis=-1, keepdims=True)
    normed = (values * lax.rsqrt(mean_square + EPSILON) * gain[...]).astype(BF16)
    out[...] = jnp.dot(placing, normed, preferred_element_type=F32).astype(BF16)
    copies[1].wait()
    sublanes = lax.broadcasted_iota(jnp.int32, (rows, slots), 0)
    wanted = jnp.zeros((rows, slots), jnp.int32)
    for r in range(rows):
        wanted = jnp.where(sublanes == r, slot[order_ref[r]], wanted)
    chosen = lax.broadcasted_iota(jnp.int32, (rows, slots), 1) == wanted
    select[...] = chosen.astype(BF16)


def dispatch(task_ids, order, tokens, gain, experts):
    rows, width = tokens.shape
    slots = experts * CAP
    arrays = (task_ids, order, tokens, gain.reshape(1, width))
    return pl.pallas_call(
        dispatch_kernel,
        out_shape=[pltpu.VMEM((slots, width), BF16), pltpu.VMEM((rows, slots), BF16)],
        in_specs=[ANYWHERE] * 4,
        out_specs=[IN_VMEM] * 2,
        scratch_shapes=[
            pltpu.VMEM((rows, width), BF16),
            pltpu.VMEM((1, width), F32),
            pltpu.SMEM((rows,), jnp.int32),
            pltpu.SMEM((rows,), jnp.int32),
            pltpu.SMEM((experts,), jnp.int32),
            pltpu.SMEM((rows,), jnp.int32),
            pltpu.SemaphoreType.DMA((4,)),
        ],
        compiler_params=pltpu.CompilerParams(vmem_limit_bytes=8 * 1024 * 1024),
        name="dispatch",
    )(*[in_hbm(v) for v in arrays])


def pick_kernel(which_ref, wg, wu, wd, og, ou, od, sem):
    which = which_ref[0]
    run_copies(
        [
            pltpu.make_async_copy(w.at[which], o, sem.at[i])
            for i, (w, o) in enumerate(((wg, og), (wu, ou), (wd, od)))
        ]
    )


def pick(which, w_gate, w_up, w_down):
    return pl.pallas_call(
        pick_kernel,
        out_shape=[pltpu.VMEM(w.shape[1:], BF16) for w in (w_gate, w_up, w_down)],
        in_specs=[pl.BlockSpec(memory_space=pltpu.SMEM)] + [ANYWHERE] * 3,
        out_specs=[IN_VMEM] * 3,
        scratch_shapes=[pltpu.SemaphoreType.DMA((3,))],
        compiler_params=pltpu.CompilerParams(vmem_limit_bytes=1024 * 1024),
        name="pick",
    )(which, in_hbm(w_gate), in_hbm(w_up), in_hbm(w_down))


def load_kernel(core_ref, wg, wpg, wu, wpu, wd, wpd, w1, w2, sem):
    core = core_ref[0]
    part = wpd.shape[0]
    run_copies(
        [
            pltpu.make_async_copy(wg.at[core], w1.at[pl.ds(0, part)], sem.at[0]),
            pltpu.make_async_copy(wpg, w1.at[pl.ds(part, part)], sem.at[1]),
            pltpu.make_async_copy(wu.at[core], w1.at[pl.ds(2 * part, part)], sem.at[2]),
            pltpu.make_async_copy(wpu, w1.at[pl.ds(3 * part, part)], sem.at[3]),
            pltpu.make_async_copy(wd.at[core], w2.at[pl.ds(0, part)], sem.at[4]),
            pltpu.make_async_copy(wpd, w2.at[pl.ds(part, part)], sem.at[5]),
        ]
    )


def load(core, *weights):
    part, width = weights[-1].shape
    return pl.pallas_call(
        load_kernel,
        out_shape=[
            pltpu.VMEM((2 * CORES * part, width), BF16),
            pltpu.VMEM((CORES * part, width), BF16),
        ],
        in_specs=[pl.BlockSpec(memory_space=pltpu.SMEM)] + [ANYWHERE] * 6,
        out_specs=[IN_VMEM] * 2,
        scratch_shapes=[pltpu.SemaphoreType.DMA((6,))],
        compiler_params=pltpu.CompilerParams(vmem_limit_bytes=1024 * 1024),
        name="load",
    )(core, *[in_hbm(w) if w.ndim == 3 else in_vmem(w) for w in weights])


def ffn_kernel(rows, looped, *refs):
    n = len(rows)
    xs, (w1, w2), outs = refs[:n], refs[n : n + 2], refs[n + 2 : 2 * n + 2]
    x, gu, h = refs[2 * n + 2 :]
    width = w1.shape[1]
    hidden = w2.shape[0]
    starts = [sum(rows[:i]) for i in range(n)]
    for i in range(n):
        x[starts[i] : starts[i] + rows[i], :] = xs[i][...]

    def gate_and_up(at):
        gu[:, at] = lax.dot_general(
            x[...], w1[at, :], (((1,), (1,)), ((), ())), preferred_element_type=F32
        )

    if looped:

        @pl.loop(0, 2 * hidden // CHUNK)
        def _(j):
            gate_and_up(pl.ds(pl.multiple_of(j * CHUNK, CHUNK), CHUNK))

    else:
        for j in range(2 * hidden // CHUNK):
            gate_and_up(slice(j * CHUNK, (j + 1) * CHUNK))

    gate = gu[:, :hidden]
    h[...] = (gate / (1.0 + jnp.exp(-gate)) * gu[:, hidden:]).astype(BF16)

    @pl.loop(0, width // WIDE)
    def _(j):
        cols = pl.ds(pl.multiple_of(j * WIDE, WIDE), WIDE)
        y = jnp.dot(h[...], w2[:, cols], preferred_element_type=F32).astype(BF16)
        for i in range(n):
            outs[i][:, cols] = y[starts[i] : starts[i] + rows[i]]


def ffn(xs, w1, w2, looped=False):
    rows = tuple(v.shape[0] for v in xs)
    total = sum(rows)
    hidden, width = w2.shape
    n = len(xs)
    return pl.pallas_call(
        functools.partial(ffn_kernel, rows, looped),
        out_shape=[pltpu.VMEM(v.shape, BF16) for v in xs],
        in_specs=[IN_VMEM] * (n + 2),
        out_specs=[IN_VMEM] * n,
        scratch_shapes=[
            pltpu.VMEM((total, width), BF16),
            pltpu.VMEM((total, 2 * hidden), F32),
            pltpu.VMEM((total, hidden), BF16),
        ],
        compiler_params=pltpu.CompilerParams(vmem_limit_bytes=10 * 1024 * 1024),
        cost_estimate=pl.CostEstimate(
            flops=6 * total * width * hidden, transcendentals=total * hidden, bytes_accessed=0
        ),
        name="ffn",
    )(*[in_vmem(v) for v in xs], in_vmem(w1), in_vmem(w2))


def ring_gather(v, axis):
    half = v.shape[0] // 2
    plus, minus = shift(v, axis, 1), shift(v, axis, -1)
    plus2, minus2 = shift(plus[:half], axis, 1), shift(minus[half:], axis, -1)
    return jnp.concatenate([v, plus, minus, plus2, minus2], axis=0)


def add(*terms):
    total = terms[0].astype(F32)
    for term in terms[1:]:
        total = total + term.astype(F32)
    return total.astype(BF16)


def ring_scatter(v, axis):
    unit = v.shape[0] // RING
    own, plus, minus, far = [v[k * unit : (k + 1) * unit] for k in range(RING)]
    far, plus, minus = shift(far, axis, 2), shift(plus, axis, -1), shift(minus, axis, 1)
    return add(own, plus, minus, far)


def first_halves(v, axis):
    half = v.shape[0] // 2
    return [shift(v[:half], axis, 1), shift(v[half:], axis, -1)]


def second_halves(v, axis):
    half = v.shape[0] // 2
    return [shift(v[half:], axis, 1), shift(v[:half], axis, -1)]


def onward(pair, axis):
    return [shift(pair[0], axis, 1), shift(pair[1], axis, -1)]


def backward(pair, axis):
    return [shift(pair[0], axis, -1), shift(pair[1], axis, 1)]


def after(*lists):
    flat = lax.optimization_barrier([v for part in lists for v in part])
    cut, out = 0, []
    for part in lists:
        out.append(flat[cut : cut + len(part)])
        cut += len(part)
    return out


def collect(own, early, late):
    half = own.shape[0] // 2
    return jnp.concatenate(
        [add(own[:half], early[1], late[0]), add(own[half:], early[0], late[1])], axis=0
    )


def layer(tokens, gain, task_ids, order, w_gate, w_up, w_down):
    local_experts = w_gate.shape[0]
    expert_count = RING * local_experts
    core = lax.axis_index("core")

    core_arg = core.astype(jnp.int32).reshape(1)
    outgoing, selecting = dispatch(task_ids, order, tokens, gain, expert_count)
    slot_count = expert_count * CAP
    per_core = slot_count // CORES
    kept, swapped = outgoing[:per_core], swap_cores(outgoing[per_core:])

    w_gate = jnp.swapaxes(w_gate, 1, 2)
    w_up = jnp.swapaxes(w_up, 1, 2)
    swapped, which = lax.optimization_barrier((swapped, 1 - core_arg))
    sent = pick(which, w_gate, w_up, w_down)
    peers = [swap_cores(w) for w in sent]

    def for_group(k):
        at = slice(k * CAP, (k + 1) * CAP)
        return jnp.concatenate([kept[at], swapped[at]], axis=0)

    groups = [for_group(0)] + [shift(for_group(k), "task", k) for k in range(1, RING)]
    a0 = ring_gather(jnp.concatenate(groups[:2], axis=0), "x")
    b0 = ring_gather(jnp.concatenate(groups[2:], axis=0), "z")
    lead_a, lead_b = first_halves(a0, "z"), first_halves(b0, "x")
    rest_a, rest_b = second_halves(a0, "z"), second_halves(b0, "x")
    (a0, b0), peers = after([a0, b0], peers)
    w1, w2 = load(core_arg, w_gate, peers[0], w_up, peers[1], w_down, peers[2])
    (w1, w2), lead_a, lead_b = after([w1, w2], lead_a, lead_b)
    far_a, far_b = onward(lead_a, "z"), onward(lead_b, "x")
    early = ffn(rest_a + rest_b, w1, w2)
    early_a, early_b = backward(early[:2], "z"), backward(early[2:], "x")
    far = ffn(far_a + far_b, w1, w2)
    far, lead_a, lead_b = after(far, lead_a, lead_b)
    far_a, far_b = backward(far[:2], "z"), backward(far[2:], "x")
    late = ffn(lead_a + lead_b, w1, w2)
    far_a, late_a = after(far_a, late[:2])
    far_b, late_b, (a0, b0) = after(far_b, late[2:], [a0, b0])
    late_a = backward([add(v, w) for v, w in zip(late_a, far_a)], "z")
    late_b = backward([add(v, w) for v, w in zip(late_b, far_b)], "x")
    y0 = ffn([a0, b0], w1, w2, looped=True)
    ya = collect(y0[0], early_a, late_a)
    yb = collect(y0[1], early_b, late_b)
    done_a = ring_scatter(ya, "x")
    done_b = ring_scatter(yb, "z")

    both = 2 * CAP
    groups = [done_a[:both], done_a[both:], done_b[:both], done_b[both:]]
    first = shift(groups[1], "task", -1)
    last = [shift(groups[k], "task", -k) for k in range(2, RING)]
    groups = [groups[0], first] + last
    kept = jnp.concatenate([v[:CAP] for v in groups], axis=0)
    swapped = swap_cores(jnp.concatenate([v[CAP:] for v in groups], axis=0))
    returned = jnp.concatenate([kept, swapped], axis=0)
    return jnp.dot(selecting, returned, preferred_element_type=F32).astype(BF16)


def solution(mesh):
    devices = mesh.devices.reshape(RING, RING, RING, CORES)
    fine = Mesh(devices, ("task", "x", "z", "core"))
    shard = ("x", "z", "core")
    every = ("task",) + shard
    placed = (
        P(every, None),
        P(),
        P(every),
        P(every),
        P("task", None, shard),
        P("task", None, shard),
        P("task", shard, None),
    )
    return jax.shard_map(
        layer, mesh=fine, in_specs=placed, out_specs=P(every, None), check_vma=False
    )
```

```python
import functools
import jax
import jax.numpy as jnp
from jax import lax
from jax.experimental import pallas as pl
from jax.experimental.pallas import tpu as pltpu
from jax.sharding import Mesh, PartitionSpec as P

CAP = 8
RING = 4
CORES = 2
EPSILON = 1e-06
F32 = jnp.float32
BF16 = jnp.bfloat16


def shift(v, axis, step):
    return lax.ppermute(v, axis, [(i, (i + step) % RING) for i in range(RING)])


def swap_cores(v):
    return lax.ppermute(v, "core", [(0, 1), (1, 0)])


CHUNK = 256
WIDE = 1024
ANYWHERE = pl.BlockSpec(memory_space=pl.ANY)
IN_VMEM = pl.BlockSpec(memory_space=pltpu.VMEM)


def in_vmem(v):
    return pltpu.with_memory_space_constraint(v, pltpu.VMEM)


def in_hbm(v):
    return pltpu.with_memory_space_constraint(v, pltpu.HBM)


def run_copies(copies):
    for copy in copies:
        copy.start()
    for copy in copies:
        copy.wait()


def dispatch_kernel(
    task_hbm, order_hbm, tokens_hbm, gain_hbm, out, select, tokens, gain, task_ref, order_ref,
    count, slot, sem,
):
    sources = (task_hbm, order_hbm, tokens_hbm, gain_hbm)
    places = (task_ref, order_ref, tokens, gain)
    copies = [
        pltpu.make_async_copy(v, w, sem.at[i]) for i, (v, w) in enumerate(zip(sources, places))
    ]
    for copy in copies:
        copy.start()
    group = lax.axis_index("task")
    core = lax.axis_index("core")
    rows = tokens.shape[0]
    slots = out.shape[0]
    experts = count.shape[0]
    for e in range(experts):
        count[e] = 0
    copies[0].wait()
    lanes = lax.broadcasted_iota(jnp.int32, (slots, rows), 1)
    targets = jnp.zeros((slots, rows), jnp.int32)
    for r in range(rows):
        task = task_ref[r]
        position = count[task]
        count[task] = position + 1
        far = (task // CORES - group) & (RING - 1)
        other = (task + core) & (CORES - 1)
        at = (other * RING + far) * CAP + position
        slot[r] = at
        targets = jnp.where(lanes == r, at, targets)
    placing = (lax.broadcasted_iota(jnp.int32, (slots, rows), 0) == targets).astype(BF16)
    copies[2].wait()
    copies[3].wait()
    values = tokens[...].astype(F32)
    mean_square = jnp.mean(values * values, axis=-1, keepdims=True)
    normed = (values * lax.rsqrt(mean_square + EPSILON) * gain[...]).astype(BF16)
    out[...] = jnp.dot(placing, normed, preferred_element_type=F32).astype(BF16)
    copies[1].wait()
    sublanes = lax.broadcasted_iota(jnp.int32, (rows, slots), 0)
    wanted = jnp.zeros((rows, slots), jnp.int32)
    for r in range(rows):
        wanted = jnp.where(sublanes == r, slot[order_ref[r]], wanted)
    chosen = lax.broadcasted_iota(jnp.int32, (rows, slots), 1) == wanted
    select[...] = chosen.astype(BF16)


def dispatch(task_ids, order, tokens, gain, experts):
    rows, width = tokens.shape
    slots = experts * CAP
    arrays = (task_ids, order, tokens, gain.reshape(1, width))
    return pl.pallas_call(
        dispatch_kernel,
        out_shape=[pltpu.VMEM((slots, width), BF16), pltpu.VMEM((rows, slots), BF16)],
        in_specs=[ANYWHERE] * 4,
        out_specs=[IN_VMEM] * 2,
        scratch_shapes=[
            pltpu.VMEM((rows, width), BF16),
            pltpu.VMEM((1, width), F32),
            pltpu.SMEM((rows,), jnp.int32),
            pltpu.SMEM((rows,), jnp.int32),
            pltpu.SMEM((experts,), jnp.int32),
            pltpu.SMEM((rows,), jnp.int32),
            pltpu.SemaphoreType.DMA((4,)),
        ],
        compiler_params=pltpu.CompilerParams(vmem_limit_bytes=8 * 1024 * 1024),
        name="dispatch",
    )(*[in_hbm(v) for v in arrays])


def pick_kernel(which_ref, wg, wu, wd, og, ou, od, sem):
    which = which_ref[0]
    run_copies(
        [
            pltpu.make_async_copy(w.at[which], o, sem.at[i])
            for i, (w, o) in enumerate(((wg, og), (wu, ou), (wd, od)))
        ]
    )


def pick(which, w_gate, w_up, w_down):
    return pl.pallas_call(
        pick_kernel,
        out_shape=[pltpu.VMEM(w.shape[1:], BF16) for w in (w_gate, w_up, w_down)],
        in_specs=[pl.BlockSpec(memory_space=pltpu.SMEM)] + [ANYWHERE] * 3,
        out_specs=[IN_VMEM] * 3,
        scratch_shapes=[pltpu.SemaphoreType.DMA((3,))],
        compiler_params=pltpu.CompilerParams(vmem_limit_bytes=1024 * 1024),
        name="pick",
    )(which, in_hbm(w_gate), in_hbm(w_up), in_hbm(w_down))


def load_kernel(core_ref, wg, wpg, wu, wpu, wd, wpd, w1, w2, sem):
    core = core_ref[0]
    part = wpd.shape[0]
    run_copies(
        [
            pltpu.make_async_copy(wg.at[core], w1.at[pl.ds(0, part)], sem.at[0]),
            pltpu.make_async_copy(wpg, w1.at[pl.ds(part, part)], sem.at[1]),
            pltpu.make_async_copy(wu.at[core], w1.at[pl.ds(2 * part, part)], sem.at[2]),
            pltpu.make_async_copy(wpu, w1.at[pl.ds(3 * part, part)], sem.at[3]),
            pltpu.make_async_copy(wd.at[core], w2.at[pl.ds(0, part)], sem.at[4]),
            pltpu.make_async_copy(wpd, w2.at[pl.ds(part, part)], sem.at[5]),
        ]
    )


def load(core, *weights):
    part, width = weights[-1].shape
    return pl.pallas_call(
        load_kernel,
        out_shape=[
            pltpu.VMEM((2 * CORES * part, width), BF16),
            pltpu.VMEM((CORES * part, width), BF16),
        ],
        in_specs=[pl.BlockSpec(memory_space=pltpu.SMEM)] + [ANYWHERE] * 6,
        out_specs=[IN_VMEM] * 2,
        scratch_shapes=[pltpu.SemaphoreType.DMA((6,))],
        compiler_params=pltpu.CompilerParams(vmem_limit_bytes=1024 * 1024),
        name="load",
    )(core, *[in_hbm(w) if w.ndim == 3 else in_vmem(w) for w in weights])


def ffn_kernel(rows, looped, *refs):
    n = len(rows)
    xs, (w1, w2), outs = refs[:n], refs[n : n + 2], refs[n + 2 : 2 * n + 2]
    x, gu, h = refs[2 * n + 2 :]
    width = w1.shape[1]
    hidden = w2.shape[0]
    starts = [sum(rows[:i]) for i in range(n)]
    for i in range(n):
        x[starts[i] : starts[i] + rows[i], :] = xs[i][...]

    def gate_and_up(at):
        gu[:, at] = lax.dot_general(
            x[...], w1[at, :], (((1,), (1,)), ((), ())), preferred_element_type=F32
        )

    if looped:

        @pl.loop(0, 2 * hidden // CHUNK)
        def _(j):
            gate_and_up(pl.ds(pl.multiple_of(j * CHUNK, CHUNK), CHUNK))

    else:
        for j in range(2 * hidden // CHUNK):
            gate_and_up(slice(j * CHUNK, (j + 1) * CHUNK))

    gate = gu[:, :hidden]
    h[...] = (gate / (1.0 + jnp.exp(-gate)) * gu[:, hidden:]).astype(BF16)

    @pl.loop(0, width // WIDE)
    def _(j):
        cols = pl.ds(pl.multiple_of(j * WIDE, WIDE), WIDE)
        y = jnp.dot(h[...], w2[:, cols], preferred_element_type=F32).astype(BF16)
        for i in range(n):
            outs[i][:, cols] = y[starts[i] : starts[i] + rows[i]]


def ffn(xs, w1, w2, looped=False):
    rows = tuple(v.shape[0] for v in xs)
    total = sum(rows)
    hidden, width = w2.shape
    n = len(xs)
    return pl.pallas_call(
        functools.partial(ffn_kernel, rows, looped),
        out_shape=[pltpu.VMEM(v.shape, BF16) for v in xs],
        in_specs=[IN_VMEM] * (n + 2),
        out_specs=[IN_VMEM] * n,
        scratch_shapes=[
            pltpu.VMEM((total, width), BF16),
            pltpu.VMEM((total, 2 * hidden), F32),
            pltpu.VMEM((total, hidden), BF16),
        ],
        compiler_params=pltpu.CompilerParams(vmem_limit_bytes=10 * 1024 * 1024),
        cost_estimate=pl.CostEstimate(
            flops=6 * total * width * hidden, transcendentals=total * hidden, bytes_accessed=0
        ),
        name="ffn",
    )(*[in_vmem(v) for v in xs], in_vmem(w1), in_vmem(w2))


def ring_gather(v, axis):
    half = v.shape[0] // 2
    plus, minus = shift(v, axis, 1), shift(v, axis, -1)
    plus2, minus2 = shift(plus[:half], axis, 1), shift(minus[half:], axis, -1)
    return jnp.concatenate([v, plus, minus, plus2, minus2], axis=0)


def add(*terms):
    total = terms[0].astype(F32)
    for term in terms[1:]:
        total = total + term.astype(F32)
    return total.astype(BF16)


def ring_scatter(v, axis):
    unit = v.shape[0] // RING
    own, plus, minus, far = [v[k * unit : (k + 1) * unit] for k in range(RING)]
    far, plus, minus = shift(far, axis, 2), shift(plus, axis, -1), shift(minus, axis, 1)
    return add(own, plus, minus, far)


def first_halves(v, axis):
    half = v.shape[0] // 2
    return [shift(v[:half], axis, 1), shift(v[half:], axis, -1)]


def second_halves(v, axis):
    half = v.shape[0] // 2
    return [shift(v[half:], axis, 1), shift(v[:half], axis, -1)]


def onward(pair, axis):
    return [shift(pair[0], axis, 1), shift(pair[1], axis, -1)]


def backward(pair, axis):
    return [shift(pair[0], axis, -1), shift(pair[1], axis, 1)]


def after(*lists):
    flat = lax.optimization_barrier([v for part in lists for v in part])
    cut, out = 0, []
    for part in lists:
        out.append(flat[cut : cut + len(part)])
        cut += len(part)
    return out


def collect(own, early, late):
    half = own.shape[0] // 2
    return jnp.concatenate(
        [add(own[:half], early[1], late[0]), add(own[half:], early[0], late[1])], axis=0
    )


def layer(tokens, gain, task_ids, order, w_gate, w_up, w_down):
    local_experts = w_gate.shape[0]
    expert_count = RING * local_experts
    core = lax.axis_index("core")

    core_arg = core.astype(jnp.int32).reshape(1)
    outgoing, selecting = dispatch(task_ids, order, tokens, gain, expert_count)
    slot_count = expert_count * CAP
    per_core = slot_count // CORES
    kept, swapped = outgoing[:per_core], swap_cores(outgoing[per_core:])

    w_gate = jnp.swapaxes(w_gate, 1, 2)
    w_up = jnp.swapaxes(w_up, 1, 2)
    swapped, which = lax.optimization_barrier((swapped, 1 - core_arg))
    sent = pick(which, w_gate, w_up, w_down)
    peers = [swap_cores(w) for w in sent]

    def for_group(k):
        at = slice(k * CAP, (k + 1) * CAP)
        return jnp.concatenate([kept[at], swapped[at]], axis=0)

    groups = [for_group(0)] + [shift(for_group(k), "task", k) for k in range(1, RING)]
    a0 = ring_gather(jnp.concatenate(groups[:2], axis=0), "x")
    b0 = ring_gather(jnp.concatenate(groups[2:], axis=0), "z")
    lead_a, lead_b = first_halves(a0, "z"), first_halves(b0, "x")
    rest_a, rest_b = second_halves(a0, "z"), second_halves(b0, "x")
    (a0, b0), peers = after([a0, b0], peers)
    w1, w2 = load(core_arg, w_gate, peers[0], w_up, peers[1], w_down, peers[2])
    (w1, w2), lead_a, lead_b = after([w1, w2], lead_a, lead_b)
    far_a, far_b = onward(lead_a, "z"), onward(lead_b, "x")
    early = ffn(rest_a + rest_b, w1, w2)
    early_a, early_b = backward(early[:2], "z"), backward(early[2:], "x")
    far = ffn(far_a + far_b, w1, w2)
    far, lead_a, lead_b = after(far, lead_a, lead_b)
    far_a, far_b = backward(far[:2], "z"), backward(far[2:], "x")
    late = ffn(lead_a + lead_b, w1, w2)
    far_a, late_a = after(far_a, late[:2])
    far_b, late_b, (a0, b0) = after(far_b, late[2:], [a0, b0])
    late_a = backward([add(v, w) for v, w in zip(late_a, far_a)], "z")
    late_b = backward([add(v, w) for v, w in zip(late_b, far_b)], "x")
    y0 = ffn([a0, b0], w1, w2)
    ya = collect(y0[0], early_a, late_a)
    yb = collect(y0[1], early_b, late_b)
    done_a = ring_scatter(ya, "x")
    done_b = ring_scatter(yb, "z")

    both = 2 * CAP
    groups = [done_a[:both], done_a[both:], done_b[:both], done_b[both:]]
    first = shift(groups[1], "task", -1)
    second = shift(groups[2], "task", -2)
    last = shift(groups[3], "task", -3)
    groups = [groups[0], first, second, last]
    kept = jnp.concatenate([v[:CAP] for v in groups], axis=0)
    swapped = swap_cores(jnp.concatenate([v[CAP:] for v in groups], axis=0))
    returned = jnp.concatenate([kept, swapped], axis=0)
    return jnp.dot(selecting, returned, preferred_element_type=F32).astype(BF16)


def solution(mesh):
    devices = mesh.devices.reshape(RING, RING, RING, CORES)
    fine = Mesh(devices, ("task", "x", "z", "core"))
    shard = ("x", "z", "core")
    every = ("task",) + shard
    placed = (
        P(every, None),
        P(),
        P(every),
        P(every),
        P("task", None, shard),
        P("task", None, shard),
        P("task", shard, None),
    )
    return jax.shard_map(
        layer, mesh=fine, in_specs=placed, out_specs=P(every, None), check_vma=False
    )
```
